32 devices in a mesh: blk: 4 (over y, core), ulysses: 8 (over z, x).
Axes of the slice: x: 2, y: 2, z: 4, core: 2. Of those that a mesh axis runs over, the one named last changes fastest.
Arguments:
- query_tokens: bfloat16 [4096, 4096], P(('blk', 'ulysses')), may hold values from -5 to 5
- key_tokens: bfloat16 [4096, 4096], P(('blk', 'ulysses')), may hold values from -5 to 5
- value_tokens: bfloat16 [4096, 4096], P(('blk', 'ulysses')), may hold values from -5 to 5
- cotangent: bfloat16 [4096, 4096], P(('blk', 'ulysses')), may hold values from -5 to 5
- block_mask: int32 [32, 32], replicated, may hold values from 0 to 1, as said below
Outputs:
- attended: bfloat16 [4096, 4096], P(('blk', 'ulysses'))
- grad_query: bfloat16 [4096, 4096], P(('blk', 'ulysses'))
- grad_key: bfloat16 [4096, 4096], P(('blk', 'ulysses'))
- grad_value: bfloat16 [4096, 4096], P(('blk', 'ulysses'))
The draws below stay inside these ranges and needn't reach their ends.
Inputs may be any that keep to these rules, and one draw needn't show every extreme that they name: block_mask is symmetric. A span is a run of 8 consecutive blocks. Inside a span, block s attends block s2 exactly when they differ by at most one. A query block attends at most one key block in each other span. The queries of one span attend keys of exactly 3 other spans, and at most 2 distinct key blocks of any other span; in every draw some pairs of spans reach 2.
All inputs are finite; a program needn't handle non-finite values.
Results may differ from the reference program's by a relative error of at most 0.0096.
Values may be sent and summed in bfloat16 or wider, within the bound.
No kernel may reach another device: no remote copies, remote signals or barrier semaphores. Data moves between devices by JAX's collectives and lax.ppermute only.
A program may use at most 128 MiB of HBM per device.

```python
import math
import jax
import jax.numpy as jnp
from jax import lax

HEADS = 32
HEAD_DIM = 128
BLOCK = 128
TOKENS = 4096
NBLOCKS = 32
SPAN_BLOCKS = 8
LINKS = 3
N_BLK = 4


def draw_query_tokens(key, part):
    shape = (TOKENS, HEADS * HEAD_DIM)
    row_scale = jnp.exp(jax.random.uniform(jax.random.fold_in(key, 3), (TOKENS, 1), minval=math.log(0.15), maxval=math.log(1.5)))
    noise = jax.random.truncated_normal(jax.random.fold_in(key, 1), -3.0, 3.0, shape)
    result = noise * row_scale
    return result.astype(jnp.bfloat16)


def draw_key_tokens(key, part):
    shape = (TOKENS, HEADS * HEAD_DIM)
    result = jax.random.truncated_normal(jax.random.fold_in(key, 2), -4.0, 4.0, shape)
    return result.astype(jnp.bfloat16)


def draw_block_mask(key, part):
    log_span = SPAN_BLOCKS.bit_length() - 1
    link_count = LINKS
    subkeys = jax.random.split(jax.random.fold_in(key, 11), 5)
    partner_high = jax.random.permutation(subkeys[0], N_BLK - 1)[:link_count].astype(jnp.int32) + 1
    free_bit = jax.random.randint(subkeys[1], (link_count,), 0, log_span)
    use_bit = jax.random.randint(subkeys[2], (link_count,), 0, 2)
    narrow = jax.random.randint(subkeys[3], (link_count,), 0, 2).at[0].set(0)
    bit_value = jnp.left_shift(jnp.ones((link_count,), jnp.int32), free_bit)
    all_bits = SPAN_BLOCKS - 1
    keep_bits = jnp.where(narrow == 1, all_bits, all_bits - bit_value)
    flip_bits = jnp.where(narrow == 1, 0, use_bit * bit_value)
    offsets = jax.random.randint(subkeys[4], (link_count, N_BLK), 0, SPAN_BLOCKS)
    blocks = jnp.arange(NBLOCKS, dtype=jnp.int32)
    span_of = blocks // SPAN_BLOCKS
    spot_of = blocks % SPAN_BLOCKS
    row_span = span_of[:, None]
    col_span = span_of[None, :]
    row_spot = spot_of[:, None]
    col_spot = spot_of[None, :]
    banded = (row_span == col_span) & (jnp.abs(row_spot - col_spot) <= 1)
    linked = banded
    for index_k in range(link_count):
        pair_id = jnp.minimum(span_of, span_of ^ partner_high[index_k])
        target = offsets[index_k][pair_id] & keep_bits[index_k]
        row_holds = spot_of & keep_bits[index_k] == target
        linked_now = (col_span == row_span ^ partner_high[index_k]) & (col_spot == row_spot ^ flip_bits[index_k]) & row_holds[:, None]
        linked = linked | linked_now
    return linked.astype(jnp.int32)


def levels(rng, dims, pieces, least, top_value):
    level, own = 1.0, jax.random.fold_in(rng, 6)
    for axis_at, blocks in pieces:
        draws = jnp.exp(jax.random.uniform(jax.random.fold_in(own, axis_at), (blocks,), jnp.float32, least / len(pieces), top_value / len(pieces)))
        level = level * jnp.repeat(draws, dims[axis_at] // blocks).reshape([-1 if axis == axis_at else 1 for axis in range(len(dims))])
    return level


def bell_draw(stream_key, dims, scale, reach, pieces=(), held_as=jnp.bfloat16):
    drawn = scale * jax.random.normal(stream_key, dims, jnp.float32)
    if pieces:
        drawn = drawn * levels(stream_key, dims, pieces, -0.22, 0.18)
    return jnp.clip(drawn, -reach, reach).astype(held_as)


def setup_inputs(seed: int = 0) -> dict:
    seeds = jax.random.split(jax.random.key(seed), 6)
    return {
        "query_tokens": draw_query_tokens(jax.random.fold_in(seeds[5], 71), 0),
        "key_tokens": draw_key_tokens(jax.random.fold_in(seeds[5], 71), 0),
        "value_tokens": bell_draw(seeds[2], (TOKENS, HEADS * HEAD_DIM), 1.0, 5.0, ((0, 32),)),
        "cotangent": bell_draw(seeds[3], (TOKENS, HEADS * HEAD_DIM), 1.0, 5.0, ((0, 32),)),
        "block_mask": draw_block_mask(jax.random.fold_in(seeds[5], 71), 0),
    }


def round_trip(tensor):
    return lax.optimization_barrier(tensor.astype(jnp.bfloat16)).astype(jnp.float32)


def head_pass(blocks, index_list, is_valid):
    queries, keyset, values, upstream = blocks
    score_scale = HEAD_DIM ** -0.5
    query_f = queries.astype(jnp.float32)
    upstream_f = upstream.astype(jnp.float32)
    key_tiles = keyset[index_list].astype(jnp.float32)
    value_tiles = values[index_list].astype(jnp.float32)
    scores = jnp.einsum('ird,itcd->itrc', query_f, key_tiles) * score_scale
    scores = jnp.where(is_valid[:, :, None, None], scores, -jnp.inf)
    row_peak = jnp.max(scores, axis=(1, 3))
    row_total = jnp.sum(jnp.exp(scores - row_peak[:, None, :, None]), axis=(1, 3))
    log_total = row_peak + jnp.log(row_total)
    probability = jnp.exp(scores - log_total[:, None, :, None])
    weights = round_trip(probability)
    output = jnp.einsum('itrc,itcd->ird', weights, value_tiles)
    row_delta = jnp.sum(upstream_f * output, axis=2)
    grad_prob = jnp.einsum('ird,itcd->itrc', upstream_f, value_tiles)
    dscore = round_trip(probability * (grad_prob - row_delta[:, None, :, None]))
    grad_q = jnp.einsum('itrc,itcd->ird', dscore, key_tiles) * score_scale
    key_terms = jnp.einsum('itrc,ird->itcd', dscore, query_f) * score_scale
    value_terms = jnp.einsum('itrc,ird->itcd', weights, upstream_f)
    grad_k = jnp.zeros_like(query_f).at[index_list].add(key_terms)
    grad_v = jnp.zeros_like(query_f).at[index_list].add(value_terms)
    return (output.astype(jnp.bfloat16), grad_q.astype(jnp.bfloat16),
            grad_k.astype(jnp.bfloat16), grad_v.astype(jnp.bfloat16))


def split_heads(tensor):
    return tensor.reshape(NBLOCKS, BLOCK, HEADS, HEAD_DIM).transpose(2, 0, 1, 3)


def merge_heads(tensor):
    return tensor.transpose(1, 2, 0, 3).reshape(TOKENS, HEADS * HEAD_DIM)


def reference(query_tokens, key_tokens, value_tokens, cotangent, block_mask):
    list_width = 3 + LINKS
    block_count = NBLOCKS
    ranking = block_mask * block_count + (block_count - 1 - lax.broadcasted_iota(jnp.int32, (block_count, block_count), 1))
    ranked, index_list = lax.top_k(ranking, list_width)
    index_list = index_list.astype(jnp.int32)
    is_valid = ranked >= block_count

    def one_head(blocks):
        return head_pass(blocks, index_list, is_valid)

    stacked = (split_heads(query_tokens), split_heads(key_tokens), split_heads(value_tokens), split_heads(cotangent))
    results = lax.map(one_head, stacked)
    return (merge_heads(results[0]), merge_heads(results[1]), merge_heads(results[2]), merge_heads(results[3]))
```

```python
import functools
import jax
import jax.numpy as jnp
from jax import lax
from jax.experimental import pallas as pl
from jax.experimental.pallas import tpu as pltpu
from jax.sharding import Mesh, PartitionSpec as P

HEAD_DIM = 128
BLOCK = 128
SUB = 2
NEG = float("-inf")
POS = float("inf")
BF16 = jnp.bfloat16
F32 = jnp.float32
SCALE = HEAD_DIM ** (-0.5)


def rows_of(slot):
    return pl.ds(pl.multiple_of(slot * BLOCK, BLOCK), BLOCK)


def head_of(h):
    return slice(h * HEAD_DIM, (h + 1) * HEAD_DIM)


def dot_nt(a, b):
    return lax.dot_general(a, b, (((1,), (1,)), ((), ())), preferred_element_type=F32)


def dot_nn(a, b):
    return lax.dot_general(a, b, (((1,), (0,)), ((), ())), preferred_element_type=F32)


def fill_pool(count, parts, pools, extra, which, sem, extra_sem):
    copies = []
    for n, (local, below, above) in enumerate(parts):
        pool = pools[n]
        start = 0
        for m, source in enumerate((local, below, above)):
            size = source.shape[0]
            copies.append(pltpu.make_async_copy(source, pool.at[pl.ds(start, size)], sem.at[n, m]))
            start += size
    for copy in copies:
        copy.start()

    def one(slot, _):
        for n, pool in enumerate(pools):
            target = pool.at[pl.ds(pl.multiple_of(start + slot * BLOCK, BLOCK), BLOCK)]
            copy = pltpu.make_async_copy(extra.at[slot, which + n], target, extra_sem)
            copy.start()
            copy.wait()
        return 0

    lax.fori_loop(0, count, one, 0)
    for copy in copies:
        copy.wait()


def query_kernel(
    width, heads, slot_ref, valid_ref, count_ref, q_ref, g_ref, k_local, v_local, below, above, extra,
    o_ref, dq_ref, stat_ref, k_pool, v_pool, sem, extra_sem,
):
    parts = (
        (k_local, below.at[0], above.at[0]),
        (v_local, below.at[1], above.at[1]),
    )
    fill_pool(count_ref[0], parts, (k_pool, v_pool), extra, 0, sem, extra_sem)
    eye = lax.broadcasted_iota(jnp.int32, (BLOCK, BLOCK), 0) == lax.broadcasted_iota(
        jnp.int32, (BLOCK, BLOCK), 1
    )

    def to_row(column):
        return jnp.sum(jnp.where(eye, column, 0.0), axis=0, keepdims=True)

    def block(i, _):
        here = rows_of(i)
        slots = [rows_of(slot_ref[i, t]) for t in range(width)]
        bias = jnp.concatenate(
            [
                jnp.full((1, BLOCK), jnp.where(valid_ref[i, t] > 0, 0.0, NEG), F32)
                for t in range(width)
            ],
            axis=1,
        )
        for h in range(heads):
            cols = head_of(h)
            q = q_ref[here, cols]
            g = g_ref[here, cols]
            keys = jnp.concatenate([k_pool[s, cols] for s in slots], axis=0)
            values = jnp.concatenate([v_pool[s, cols] for s in slots], axis=0)
            scores = dot_nt(q, keys) * SCALE + bias
            peak = jnp.max(scores, axis=1, keepdims=True)
            prob = jnp.exp(scores - peak)
            total = jnp.sum(prob, axis=1, keepdims=True)
            prob = prob * (1.0 / total)
            out = dot_nn(prob.astype(BF16), values)
            delta = jnp.sum(g.astype(F32) * out, axis=1, keepdims=True)
            dprob = dot_nt(g, values)
            dscore = (prob * (dprob - delta)).astype(BF16)
            o_ref[here, cols] = out.astype(BF16)
            dq_ref[here, cols] = (dot_nn(dscore, keys) * SCALE).astype(BF16)
            stat_ref[i, 0, pl.ds(h, 1), :] = to_row(peak + jnp.log(total))
            stat_ref[i, 1, pl.ds(h, 1), :] = to_row(delta)
        return 0

    lax.fori_loop(0, q_ref.shape[0] // BLOCK, block, 0)


def key_kernel(
    width, heads, slot_ref, valid_ref, place_ref, count_ref, k_ref, v_ref, stat_ref, q_local, g_local,
    below, above, extra, dk_ref, dv_ref, q_pool, g_pool, sem, extra_sem,
):
    parts = (
        (q_local, below.at[0], above.at[0]),
        (g_local, below.at[1], above.at[1]),
    )
    fill_pool(count_ref[0], parts, (q_pool, g_pool), extra, 2, sem, extra_sem)

    def block(j, _):
        here = rows_of(j)
        slots = [rows_of(slot_ref[j, t]) for t in range(width)]
        for h in range(heads):
            cols = head_of(h)
            k = k_ref[here, cols]
            v = v_ref[here, cols]
            queries = jnp.concatenate([q_pool[s, cols] for s in slots], axis=0)
            upstream = jnp.concatenate([g_pool[s, cols] for s in slots], axis=0)
            log_row = jnp.concatenate(
                [
                    jnp.where(valid_ref[j, t] > 0, stat_ref[place_ref[j, t], 0, pl.ds(h, 1), :], POS)
                    for t in range(width)
                ],
                axis=1,
            )
            delta_row = jnp.concatenate(
                [stat_ref[place_ref[j, t], 1, pl.ds(h, 1), :] for t in range(width)], axis=1
            )
            prob = jnp.exp(dot_nt(k, queries) * SCALE - log_row)
            dprob = dot_nt(v, upstream)
            dscore = (prob * (dprob - delta_row)).astype(BF16)
            dv_ref[here, cols] = dot_nn(prob.astype(BF16), upstream).astype(BF16)
            dk_ref[here, cols] = (dot_nn(dscore, queries) * SCALE).astype(BF16)
        return 0

    lax.fori_loop(0, k_ref.shape[0] // BLOCK, block, 0)


def tables(block_mask, spans, span_len, steps):
    z = lax.axis_index("z")
    local = spans * SUB
    iota = functools.partial(lax.broadcasted_iota, jnp.int32)
    cube = block_mask.reshape(spans, span_len, spans, span_len)
    spot = iota(cube.shape, 3)
    partner = jnp.sum(cube * (spot + 1), axis=3) - 1
    shape = partner.shape
    mine, spot, other = iota(shape, 0), iota(shape, 1), iota(shape, 2)
    linked = (partner >= 0) & (mine != other)
    hop = jnp.where(linked, (partner // SUB) ^ (spot // SUB), 0)
    per_place = hop.reshape(spans, steps, SUB, spans)
    rounds = [
        jnp.max(jnp.sum((per_place == d).astype(jnp.int32), axis=(0, 2, 3))) for d in range(1, steps)
    ]
    key = jnp.where(
        mine < other,
        (mine * span_len + spot) * spans + other,
        (other * span_len + partner) * spans + mine,
    )

    def at_place(table):
        return lax.dynamic_slice_in_dim(table, z * SUB, SUB, 1).reshape(local, spans)

    partner_l, linked_l, hop_l, key_l = at_place(partner), at_place(linked), at_place(hop), at_place(key)
    other_l, mine_l = at_place(other), at_place(mine)
    block_l = iota((local, spans), 0)
    order = (hop_l * (spans * span_len * spans) + key_l).reshape(-1)
    crossing = (hop_l > 0).reshape(-1)
    earlier = crossing[None, :] & (order[None, :] < order[:, None])
    extra_slot = jnp.sum(earlier.astype(jnp.int32), axis=1)
    capacity = spans * (spans - 1)
    hits = crossing[:, None] & (extra_slot[:, None] == iota((local * spans, capacity), 1))
    send_block = jnp.sum(hits.astype(jnp.int32) * block_l.reshape(-1)[:, None], axis=0)
    counts = jnp.stack([jnp.sum((hop_l == d).astype(jnp.int32)) for d in range(1, steps)])
    count = jnp.sum(counts)
    cross_slot = jnp.where(
        hop_l > 0,
        local + 2 * spans + extra_slot.reshape(local, spans),
        other_l * SUB + partner_l % SUB,
    )
    cross_place = (partner_l // SUB) * local + other_l * SUB + partner_l % SUB
    own = block_l[:, :1]
    span_l, x_l = own // SUB, own % SUB
    left_slot = jnp.where(x_l > 0, own - 1, local + span_l)
    right_slot = jnp.where(x_l < SUB - 1, own + 1, local + spans + span_l)
    left_ok = (x_l > 0) | (z > 0)
    right_ok = (x_l < SUB - 1) | (z < steps - 1)
    own_place = z * local + own
    left_place = jnp.where(x_l > 0, own_place - 1, (z - 1) * local + span_l * SUB + SUB - 1)
    right_place = jnp.where(x_l < SUB - 1, own_place + 1, (z + 1) * local + span_l * SUB)
    turn = (mine_l + 1 + iota((local, spans), 1)) % spans

    def pick(table):
        chosen = turn[:, :, None] == iota((local, spans, spans), 2)
        return jnp.sum(jnp.where(chosen, table[:, None, :], 0), axis=2)[:, : spans - 1]

    ok = jnp.concatenate(
        [jnp.ones_like(own), left_ok.astype(jnp.int32), right_ok.astype(jnp.int32), pick(linked_l.astype(jnp.int32))],
        axis=1,
    )
    slot = jnp.where(ok > 0, jnp.concatenate([own, left_slot, right_slot, pick(cross_slot)], axis=1), own)
    place = jnp.where(
        ok > 0, jnp.concatenate([own_place, left_place, right_place, pick(cross_place)], axis=1), own_place
    )
    return slot, ok, place, count, counts, rounds, send_block, capacity


def shards(query_tokens, key_tokens, value_tokens, cotangent, block_mask):
    spans = lax.axis_size("blk")
    steps = lax.axis_size("z")
    span_len = steps * SUB
    local = spans * SUB

    def to_heads(tensor):
        return lax.all_to_all(tensor, ("blk", "x"), split_axis=1, concat_axis=0, tiled=True)

    def to_tokens(tensor):
        return lax.all_to_all(tensor, ("blk", "x"), split_axis=0, concat_axis=1, tiled=True)

    q, k, v, g = [to_heads(t) for t in (query_tokens, key_tokens, value_tokens, cotangent)]
    columns = q.shape[1]
    heads = columns // HEAD_DIM
    slot, ok, place, count, counts, rounds, send_block, capacity = tables(
        block_mask, spans, span_len, steps
    )
    width = slot.shape[1]

    def edge(tensor, x):
        return tensor.reshape(spans, SUB, BLOCK, columns)[:, x].reshape(spans * BLOCK, columns)

    upward = [(n, n + 1) for n in range(steps - 1)]
    downward = [(n + 1, n) for n in range(steps - 1)]

    def neighbours(first, second):
        below = lax.ppermute(jnp.stack([edge(first, SUB - 1), edge(second, SUB - 1)]), "z", upward)
        above = lax.ppermute(jnp.stack([edge(first, 0), edge(second, 0)]), "z", downward)
        return below, above

    kv_below, kv_above = neighbours(k, v)
    qg_below, qg_above = neighbours(q, g)

    extra = pl.pallas_call(
        lambda out_ref: None,
        out_shape=jax.ShapeDtypeStruct((capacity + 1, 4, BLOCK, columns), BF16),
        out_specs=pl.BlockSpec(memory_space=pl.ANY),
        name="extra_blocks",
    )()
    first = jnp.int32(0)
    for d in range(1, steps):
        swap = [(n, n ^ d) for n in range(steps)]
        mine = counts[d - 1]

        def one_round(r, buffer, swap=swap, first=first, mine=mine):
            at = jnp.where(r < mine, first + r, capacity)
            start = send_block[jnp.minimum(at, capacity - 1)] * BLOCK
            sent = jnp.stack([lax.dynamic_slice_in_dim(t, start, BLOCK, 0) for t in (k, v, q, g)])
            got = lax.ppermute(sent, "z", swap)
            return lax.dynamic_update_slice_in_dim(buffer, got[None], at, 0)

        extra = lax.fori_loop(0, rounds[d - 1], one_round, extra)
        first = first + mine
    count = count.reshape(1)

    rows = local * BLOCK
    pool = (rows + 2 * spans * BLOCK + capacity * BLOCK, columns)
    smem = pl.BlockSpec(memory_space=pltpu.SMEM)
    vmem = pl.BlockSpec(memory_space=pltpu.VMEM)
    anywhere = pl.BlockSpec(memory_space=pl.ANY)
    scratch = [
        pltpu.VMEM(pool, BF16),
        pltpu.VMEM(pool, BF16),
        pltpu.SemaphoreType.DMA((2, 3)),
        pltpu.SemaphoreType.DMA,
    ]
    flops = 2 * 4 * local * heads * width * BLOCK * BLOCK * HEAD_DIM
    cost = pl.CostEstimate(
        flops=flops, bytes_accessed=16 * rows * columns, transcendentals=local * heads * width * BLOCK * BLOCK
    )
    out, grad_q, stats = pl.pallas_call(
        functools.partial(query_kernel, width, heads),
        out_shape=(
            jax.ShapeDtypeStruct((rows, columns), BF16),
            jax.ShapeDtypeStruct((rows, columns), BF16),
            jax.ShapeDtypeStruct((local, 2, heads, BLOCK), F32),
        ),
        in_specs=[smem, smem, smem, vmem, vmem] + [anywhere] * 5,
        out_specs=(vmem, vmem, vmem),
        scratch_shapes=scratch,
        cost_estimate=cost,
        name="query_pass",
    )(slot, ok, count, q, g, k, v, kv_below, kv_above, extra)
    spread = jnp.broadcast_to(stats[None], (steps,) + stats.shape)
    all_stats = lax.all_to_all(spread, "z", split_axis=0, concat_axis=0, tiled=True)
    all_stats = all_stats.reshape(steps * local, 2, heads, BLOCK)
    grad_k, grad_v = pl.pallas_call(
        functools.partial(key_kernel, width, heads),
        out_shape=(
            jax.ShapeDtypeStruct((rows, columns), BF16),
            jax.ShapeDtypeStruct((rows, columns), BF16),
        ),
        in_specs=[smem, smem, smem, smem, vmem, vmem, vmem] + [anywhere] * 5,
        out_specs=(vmem, vmem),
        scratch_shapes=scratch,
        cost_estimate=cost,
        name="key_pass",
    )(slot, ok, place, count, k, v, all_stats, q, g, qg_below, qg_above, extra)
    return to_tokens(out), to_tokens(grad_q), to_tokens(grad_k), to_tokens(grad_v)


def solution(mesh):
    spans, ulysses = mesh.shape["blk"], mesh.shape["ulysses"]
    split = Mesh(mesh.devices.reshape(spans, ulysses // SUB, SUB), ("blk", "z", "x"))
    tokens = P(("blk", "z", "x"), None)
    return jax.shard_map(
        shards,
        mesh=split,
        in_specs=(tokens, tokens, tokens, tokens, P()),
        out_specs=(tokens, tokens, tokens, tokens),
        check_vma=False,
    )
```

```python
import functools
import jax
import jax.numpy as jnp
from jax import lax
from jax.experimental import pallas as pl
from jax.experimental.pallas import tpu as pltpu
from jax.sharding import Mesh, PartitionSpec as P

HEAD_DIM = 128
BLOCK = 128
SUB = 2
NEG = float("-inf")
POS = float("inf")
BF16 = jnp.bfloat16
F32 = jnp.float32
SCALE = HEAD_DIM ** (-0.5)


def head_of(h):
    return slice(h * HEAD_DIM, (h + 1) * HEAD_DIM)


def dot_nt(a, b):
    return lax.dot_general(a, b, (((1,), (1,)), ((), ())), preferred_element_type=F32)


def dot_nn(a, b):
    return lax.dot_general(a, b, (((1,), (0,)), ((), ())), preferred_element_type=F32)


def pack_kernel(a_ref, b_ref, out_ref, held, in_sem, out_sem):
    groups, _, _, columns = out_ref.shape
    arrive, leave = [], []
    for c in range(groups):
        for n, source in enumerate((a_ref, b_ref)):
            arrive.append(
                pltpu.make_async_copy(
                    source.at[:, c * columns : (c + 1) * columns], held.at[c, n], in_sem.at[c, n]
                )
            )
            leave.append(pltpu.make_async_copy(held.at[c, n], out_ref.at[c, n], out_sem.at[c, n]))
    for copy in arrive:
        copy.start()
    for first, second in zip(arrive, leave):
        first.wait()
        second.start()
    for copy in leave:
        copy.wait()


def unpack_kernel(in_ref, a_ref, b_ref, held, in_sem, out_sem):
    groups, _, _, columns = in_ref.shape
    arrive, leave = [], []
    for c in range(groups):
        for n, target in enumerate((a_ref, b_ref)):
            arrive.append(pltpu.make_async_copy(in_ref.at[c, n], held.at[c, n], in_sem.at[c, n]))
            leave.append(
                pltpu.make_async_copy(
                    held.at[c, n], target.at[:, c * columns : (c + 1) * columns], out_sem.at[c, n]
                )
            )
    for copy in arrive:
        copy.start()
    for first, second in zip(arrive, leave):
        first.wait()
        second.start()
    for copy in leave:
        copy.wait()


def pack(a, b, groups):
    rows, columns = a.shape
    shape = (groups, 2, rows, columns // groups)
    anywhere = pl.BlockSpec(memory_space=pl.ANY)
    return pl.pallas_call(
        pack_kernel,
        out_shape=jax.ShapeDtypeStruct(shape, a.dtype),
        in_specs=[anywhere] * 2,
        out_specs=anywhere,
        scratch_shapes=[
            pltpu.VMEM(shape, a.dtype),
            pltpu.SemaphoreType.DMA((groups, 2)),
            pltpu.SemaphoreType.DMA((groups, 2)),
        ],
        name="pack",
    )(a, b)


def unpack(pair):
    groups, _, rows, columns = pair.shape
    anywhere = pl.BlockSpec(memory_space=pl.ANY)
    flat = jax.ShapeDtypeStruct((rows, groups * columns), pair.dtype)
    return pl.pallas_call(
        unpack_kernel,
        out_shape=(flat, flat),
        in_specs=[anywhere],
        out_specs=(anywhere, anywhere),
        scratch_shapes=[
            pltpu.VMEM(pair.shape, pair.dtype),
            pltpu.SemaphoreType.DMA((groups, 2)),
            pltpu.SemaphoreType.DMA((groups, 2)),
        ],
        name="unpack",
    )(pair)


def fill_pool(count, parts, pool, extra, which, sem, extra_sem):
    copies = []
    start = 0
    for m, source in enumerate(parts):
        size = source.shape[0]
        copies.append(pltpu.make_async_copy(source, pool.at[pl.ds(start, size)], sem.at[m]))
        start += size
    for copy in copies:
        copy.start()

    def move(slot):
        return pltpu.make_async_copy(extra.at[slot, which], pool.at[start + slot], extra_sem.at[slot])

    lax.fori_loop(0, count, lambda slot, _: (move(slot).start(), 0)[1], 0)
    for copy in copies:
        copy.wait()
    lax.fori_loop(0, count, lambda slot, _: (move(slot).wait(), 0)[1], 0)


def by_width(cross, width, body):
    narrow = min(4, width)
    if narrow == width:
        body(width)
        return

    @pl.when(cross < 2)
    def _():
        body(narrow)

    @pl.when(cross >= 2)
    def _():
        body(width)


def query_kernel(
    width, heads, slot_ref, valid_ref, cross_ref, count_ref, qg_ref, kv_local, below, above, extra,
    out_ref, stat_ref, pool, sem, extra_sem,
):
    fill_pool(count_ref[0], (kv_local, below, above), pool, extra, 0, sem, extra_sem)
    eye = lax.broadcasted_iota(jnp.int32, (BLOCK, BLOCK), 0) == lax.broadcasted_iota(
        jnp.int32, (BLOCK, BLOCK), 1
    )

    def to_row(column):
        return jnp.sum(jnp.where(eye, column, 0.0), axis=0, keepdims=True)

    def block(i, _):
        def body(count):
            slots = [slot_ref[i, t] for t in range(count)]
            bias = jnp.concatenate(
                [
                    jnp.full((1, BLOCK), jnp.where(valid_ref[i, t] > 0, 0.0, NEG), F32)
                    for t in range(count)
                ],
                axis=1,
            )
            for h in range(heads):
                cols = head_of(h)
                q = qg_ref[i, 0, :, cols]
                g = qg_ref[i, 1, :, cols]
                keys = jnp.concatenate([pool[s, 0, :, cols] for s in slots], axis=0)
                values = jnp.concatenate([pool[s, 1, :, cols] for s in slots], axis=0)
                scores = dot_nt(q, keys) * SCALE + bias
                peak = jnp.max(scores, axis=1, keepdims=True)
                prob = jnp.exp(scores - peak)
                total = jnp.sum(prob, axis=1, keepdims=True)
                prob = prob * (1.0 / total)
                out = dot_nn(prob.astype(BF16), values)
                delta = jnp.sum(g.astype(F32) * out, axis=1, keepdims=True)
                dprob = dot_nt(g, values)
                dscore = (prob * (dprob - delta)).astype(BF16)
                out_ref[i, 0, :, cols] = out.astype(BF16)
                out_ref[i, 1, :, cols] = (dot_nn(dscore, keys) * SCALE).astype(BF16)
                stat_ref[i, 0, pl.ds(h, 1), :] = to_row(peak + jnp.log(total))
                stat_ref[i, 1, pl.ds(h, 1), :] = to_row(delta)

        by_width(cross_ref[i], width, body)
        return 0

    lax.fori_loop(0, qg_ref.shape[0], block, 0)


def key_kernel(
    width, heads, slot_ref, valid_ref, place_ref, cross_ref, count_ref, kv_ref, stat_ref, qg_local,
    below, above, extra, out_ref, pool, sem, extra_sem,
):
    fill_pool(count_ref[0], (qg_local, below, above), pool, extra, 1, sem, extra_sem)

    def block(j, _):
        def body(count):
            slots = [slot_ref[j, t] for t in range(count)]
            places = [place_ref[j, t] for t in range(count)]
            for h in range(heads):
                cols = head_of(h)
                k = kv_ref[j, 0, :, cols]
                v = kv_ref[j, 1, :, cols]
                queries = jnp.concatenate([pool[s, 0, :, cols] for s in slots], axis=0)
                upstream = jnp.concatenate([pool[s, 1, :, cols] for s in slots], axis=0)
                log_row = jnp.concatenate(
                    [
                        jnp.where(valid_ref[j, t] > 0, stat_ref[places[t], 0, pl.ds(h, 1), :], POS)
                        for t in range(count)
                    ],
                    axis=1,
                )
                delta_row = jnp.concatenate(
                    [stat_ref[places[t], 1, pl.ds(h, 1), :] for t in range(count)], axis=1
                )
                prob = jnp.exp(dot_nt(k, queries) * SCALE - log_row)
                dprob = dot_nt(v, upstream)
                dscore = (prob * (dprob - delta_row)).astype(BF16)
                out_ref[j, 1, :, cols] = dot_nn(prob.astype(BF16), upstream).astype(BF16)
                out_ref[j, 0, :, cols] = (dot_nn(dscore, queries) * SCALE).astype(BF16)

        by_width(cross_ref[j], width, body)
        return 0

    lax.fori_loop(0, kv_ref.shape[0], block, 0)


def tables(block_mask, spans, span_len, steps):
    z = lax.axis_index("z")
    local = spans * SUB
    iota = functools.partial(lax.broadcasted_iota, jnp.int32)
    cube = block_mask.reshape(spans, span_len, spans, span_len)
    spot = iota(cube.shape, 3)
    partner = jnp.sum(cube * (spot + 1), axis=3) - 1
    shape = partner.shape
    mine, spot, other = iota(shape, 0), iota(shape, 1), iota(shape, 2)
    linked = (partner >= 0) & (mine != other)
    hop = jnp.where(linked, (partner // SUB) ^ (spot // SUB), 0)
    per_place = hop.reshape(spans, steps, SUB, spans)
    rounds = [
        jnp.max(jnp.sum((per_place == d).astype(jnp.int32), axis=(0, 2, 3))) for d in range(1, steps)
    ]
    key = jnp.where(
        mine < other,
        (mine * span_len + spot) * spans + other,
        (other * span_len + partner) * spans + mine,
    )

    def at_place(table):
        return lax.dynamic_slice_in_dim(table, z * SUB, SUB, 1).reshape(local, spans)

    partner_l, linked_l, hop_l, key_l = at_place(partner), at_place(linked), at_place(hop), at_place(key)
    other_l = at_place(other)
    block_l = iota((local, spans), 0)
    order = (hop_l * (spans * span_len * spans) + key_l).reshape(-1)
    crossing = (hop_l > 0).reshape(-1)
    earlier = crossing[None, :] & (order[None, :] < order[:, None])
    extra_slot = jnp.sum(earlier.astype(jnp.int32), axis=1)
    capacity = spans * (spans - 1)
    hits = crossing[:, None] & (extra_slot[:, None] == iota((local * spans, capacity), 1))
    send_block = jnp.sum(hits.astype(jnp.int32) * block_l.reshape(-1)[:, None], axis=0)
    counts = jnp.stack([jnp.sum((hop_l == d).astype(jnp.int32)) for d in range(1, steps)])
    count = jnp.sum(counts)
    cross_slot = jnp.where(
        hop_l > 0,
        local + 2 * spans + extra_slot.reshape(local, spans),
        other_l * SUB + partner_l % SUB,
    )
    cross_place = (partner_l // SUB) * local + other_l * SUB + partner_l % SUB
    own = block_l[:, :1]
    span_l, x_l = own // SUB, own % SUB
    left_slot = jnp.where(x_l > 0, own - 1, local + span_l)
    right_slot = jnp.where(x_l < SUB - 1, own + 1, local + spans + span_l)
    left_ok = (x_l > 0) | (z > 0)
    right_ok = (x_l < SUB - 1) | (z < steps - 1)
    own_place = z * local + own
    left_place = jnp.where(x_l > 0, own_place - 1, (z - 1) * local + span_l * SUB + SUB - 1)
    right_place = jnp.where(x_l < SUB - 1, own_place + 1, (z + 1) * local + span_l * SUB)
    before = iota((local, spans, spans), 2) < iota((local, spans, spans), 1)
    rank = jnp.sum((linked_l[:, None, :] & before).astype(jnp.int32), axis=2)
    chosen = linked_l[:, None, :] & (rank[:, None, :] == iota((local, spans - 1, spans), 1))

    def pick(table):
        return jnp.sum(jnp.where(chosen, table[:, None, :], 0), axis=2)

    ok = jnp.concatenate(
        [jnp.ones_like(own), left_ok.astype(jnp.int32), right_ok.astype(jnp.int32), pick(linked_l.astype(jnp.int32))],
        axis=1,
    )
    slot = jnp.where(ok > 0, jnp.concatenate([own, left_slot, right_slot, pick(cross_slot)], axis=1), own)
    place = jnp.where(
        ok > 0, jnp.concatenate([own_place, left_place, right_place, pick(cross_place)], axis=1), own_place
    )
    cross = jnp.sum(linked_l.astype(jnp.int32), axis=1)
    return slot, ok, place, cross, count, counts, rounds, send_block, capacity


def shards(query_tokens, key_tokens, value_tokens, cotangent, block_mask):
    spans = lax.axis_size("blk")
    steps = lax.axis_size("z")
    span_len = steps * SUB
    local = spans * SUB

    def exchange(pair):
        return lax.all_to_all(pair, ("blk", "x"), split_axis=0, concat_axis=0, tiled=True)

    kv = exchange(pack(key_tokens, value_tokens, local))
    qg = exchange(pack(query_tokens, cotangent, local))
    columns = kv.shape[3]
    heads = columns // HEAD_DIM
    slot, ok, place, cross, count, counts, rounds, send_block, capacity = tables(
        block_mask, spans, span_len, steps
    )
    width = slot.shape[1]
    upward = [(n, n + 1) for n in range(steps - 1)]
    downward = [(n + 1, n) for n in range(steps - 1)]

    def neighbours(pair):
        edges = pair.reshape(spans, SUB, 2, BLOCK, columns)
        below = lax.ppermute(edges[:, SUB - 1], "z", upward)
        above = lax.ppermute(edges[:, 0], "z", downward)
        return below, above

    kv_below, kv_above = neighbours(kv)
    qg_below, qg_above = neighbours(qg)

    extra = pl.pallas_call(
        lambda out_ref: None,
        out_shape=jax.ShapeDtypeStruct((capacity + 1, 2, 2, BLOCK, columns), BF16),
        out_specs=pl.BlockSpec(memory_space=pl.ANY),
        name="extra_blocks",
    )()
    first = jnp.int32(0)
    for d in range(1, steps):
        swap = [(n, n ^ d) for n in range(steps)]
        mine = counts[d - 1]

        def one_round(r, buffer, swap=swap, first=first, mine=mine):
            at = jnp.where(r < mine, first + r, capacity)
            start = send_block[jnp.minimum(at, capacity - 1)]
            sent = jnp.concatenate([lax.dynamic_slice_in_dim(t, start, 1, 0) for t in (kv, qg)])
            got = lax.ppermute(sent, "z", swap)
            return lax.dynamic_update_slice_in_dim(buffer, got[None], at, 0)

        extra = lax.fori_loop(0, rounds[d - 1], one_round, extra)
        first = first + mine
    count = count.reshape(1)

    smem = pl.BlockSpec(memory_space=pltpu.SMEM)
    vmem = pl.BlockSpec(memory_space=pltpu.VMEM)
    anywhere = pl.BlockSpec(memory_space=pl.ANY)
    scratch = [
        pltpu.VMEM((local + 2 * spans + capacity, 2, BLOCK, columns), BF16),
        pltpu.SemaphoreType.DMA((3,)),
        pltpu.SemaphoreType.DMA((capacity,)),
    ]
    cost = pl.CostEstimate(
        flops=2 * 4 * local * heads * width * BLOCK * BLOCK * HEAD_DIM,
        bytes_accessed=16 * local * BLOCK * columns,
        transcendentals=local * heads * width * BLOCK * BLOCK,
    )
    stat_shape = (local, 2, heads, BLOCK)
    out_pair, stats = pl.pallas_call(
        functools.partial(query_kernel, width, heads),
        out_shape=(
            jax.ShapeDtypeStruct(qg.shape, BF16),
            jax.ShapeDtypeStruct(stat_shape, F32),
        ),
        in_specs=[smem] * 4 + [vmem] + [anywhere] * 4,
        out_specs=(vmem, vmem),
        scratch_shapes=scratch,
        cost_estimate=cost,
        name="query_pass",
    )(slot, ok, cross, count, qg, kv, kv_below, kv_above, extra)
    spread = jnp.broadcast_to(stats[None], (steps,) + stats.shape)
    all_stats = lax.all_to_all(spread, "z", split_axis=0, concat_axis=0, tiled=True)
    all_stats = all_stats.reshape(steps * local, 2, heads, BLOCK)
    grad_pair = pl.pallas_call(
        functools.partial(key_kernel, width, heads),
        out_shape=jax.ShapeDtypeStruct(kv.shape, BF16),
        in_specs=[smem] * 5 + [vmem, vmem] + [anywhere] * 4,
        out_specs=vmem,
        scratch_shapes=scratch,
        cost_estimate=cost,
        name="key_pass",
    )(slot, ok, place, cross, count, kv, all_stats, qg, qg_below, qg_above, extra)
    attended, grad_query = unpack(exchange(out_pair))
    grad_key, grad_value = unpack(exchange(grad_pair))
    return attended, grad_query, grad_key, grad_value


def solution(mesh):
    spans, ulysses = mesh.shape["blk"], mesh.shape["ulysses"]
    split = Mesh(mesh.devices.reshape(spans, ulysses // SUB, SUB), ("blk", "z", "x"))
    tokens = P(("blk", "z", "x"), None)
    return jax.shard_map(
        shards,
        mesh=split,
        in_specs=(tokens, tokens, tokens, tokens, P()),
        out_specs=(tokens, tokens, tokens, tokens),
        check_vma=False,
    )
```

```python
import functools
import math
import jax
import jax.numpy as jnp
from jax import lax
from jax.experimental import pallas as pl
from jax.experimental.pallas import tpu as pltpu
from jax.sharding import Mesh, PartitionSpec as P

HEAD_DIM = 128
BLOCK = 128
SUB = 2
NEG = float("-inf")
POS = float("inf")
BF16 = jnp.bfloat16
F32 = jnp.float32
SCALE = HEAD_DIM ** (-0.5)
SCALE2 = SCALE * math.log2(math.e)
OWN = 3


def head_of(h):
    return slice(h * HEAD_DIM, (h + 1) * HEAD_DIM)


def dot_nt(a, b):
    return lax.dot_general(a, b, (((1,), (1,)), ((), ())), preferred_element_type=F32)


def dot_nn(a, b):
    return lax.dot_general(a, b, (((1,), (0,)), ((), ())), preferred_element_type=F32)


def pack_kernel(a_ref, b_ref, out_ref, sem):
    groups, _, _, columns = out_ref.shape
    copies = [
        pltpu.make_async_copy(
            source.at[:, c * columns : (c + 1) * columns], out_ref.at[c, n], sem.at[c, n]
        )
        for c in range(groups)
        for n, source in enumerate((a_ref, b_ref))
    ]
    for copy in copies:
        copy.start()
    for copy in copies:
        copy.wait()


def unpack_kernel(in_ref, a_ref, b_ref, sem):
    groups, _, _, columns = in_ref.shape
    copies = [
        pltpu.make_async_copy(
            in_ref.at[c, n], target.at[:, c * columns : (c + 1) * columns], sem.at[c, n]
        )
        for c in range(groups)
        for n, target in enumerate((a_ref, b_ref))
    ]
    for copy in copies:
        copy.start()
    for copy in copies:
        copy.wait()


def pack(a, b, groups):
    rows, columns = a.shape
    anywhere = pl.BlockSpec(memory_space=pl.ANY)
    return pl.pallas_call(
        pack_kernel,
        out_shape=jax.ShapeDtypeStruct((groups, 2, rows, columns // groups), a.dtype),
        in_specs=[anywhere] * 2,
        out_specs=pl.BlockSpec(memory_space=pltpu.VMEM),
        scratch_shapes=[pltpu.SemaphoreType.DMA((groups, 2))],
        name="pack",
    )(a, b)


def unpack(pair):
    groups, _, rows, columns = pair.shape
    anywhere = pl.BlockSpec(memory_space=pl.ANY)
    flat = jax.ShapeDtypeStruct((rows, groups * columns), pair.dtype)
    return pl.pallas_call(
        unpack_kernel,
        out_shape=(flat, flat),
        in_specs=[pl.BlockSpec(memory_space=pltpu.VMEM)],
        out_specs=(anywhere, anywhere),
        scratch_shapes=[pltpu.SemaphoreType.DMA((groups, 2))],
        name="unpack",
    )(pair)


def fill_pool(count, parts, pool, extra, sem, extra_sem):
    copies = []
    start = 0
    for m, source in enumerate(parts):
        size = source.shape[0]
        copies.append(pltpu.make_async_copy(source, pool.at[pl.ds(start, size)], sem.at[m]))
        start += size
    for copy in copies:
        copy.start()

    def move(slot):
        return pltpu.make_async_copy(extra.at[slot], pool.at[start + slot], extra_sem.at[slot])

    lax.fori_loop(0, count, lambda slot, _: (move(slot).start(), 0)[1], 0)
    for copy in copies:
        copy.wait()
    lax.fori_loop(0, count, lambda slot, _: (move(slot).wait(), 0)[1], 0)


def by_width(cross, width, body):
    top = min(OWN, width - OWN)
    for n in range(top):

        @pl.when(cross == n)
        def _(n=n):
            body(OWN + n)

    @pl.when(cross >= top)
    def _():
        body(width)


def unsure(t):
    return t == OWN - 1 or t >= 2 * OWN


def query_kernel(
    width, heads, slot_ref, valid_ref, cross_ref, count_ref, qg_ref, kv_local, below, above, extra,
    out_ref, stat_ref, pool, sem, extra_sem,
):
    fill_pool(count_ref[0], (kv_local, below, above), pool, extra, sem, extra_sem)
    lane = lax.broadcasted_iota(jnp.int32, (BLOCK, BLOCK), 1)

    def block(i, _):
        def body(count):
            slots = [slot_ref[i, t] for t in range(count)]
            bias = jnp.concatenate(
                [
                    jnp.full((1, BLOCK), jnp.where(valid_ref[i, t] > 0, 0.0, NEG), F32)
                    if unsure(t)
                    else jnp.zeros((1, BLOCK), F32)
                    for t in range(count)
                ],
                axis=1,
            )
            every = range(heads)
            keys = [jnp.concatenate([pool[s, 0, :, head_of(h)] for s in slots], axis=0) for h in every]
            values = [jnp.concatenate([pool[s, 1, :, head_of(h)] for s in slots], axis=0) for h in every]
            upstream = [qg_ref[i, 1, :, head_of(h)] for h in every]
            scores = [dot_nt(qg_ref[i, 0, :, head_of(h)], keys[h]) * SCALE2 + bias for h in every]
            dprobs = [dot_nt(upstream[h], values[h]) for h in every]
            peaks = [jnp.max(scores[h], axis=1, keepdims=True) for h in every]
            probs = [jnp.exp2(scores[h] - peaks[h]) for h in every]
            totals = [jnp.sum(probs[h], axis=1, keepdims=True) for h in every]
            scales = [1.0 / totals[h] for h in every]
            outs = [dot_nn(probs[h].astype(BF16), values[h]) * scales[h] for h in every]
            deltas = [
                jnp.sum(upstream[h].astype(F32) * outs[h], axis=1, keepdims=True) for h in every
            ]
            dscores = [(probs[h] * (dprobs[h] - deltas[h])).astype(BF16) for h in every]
            grads = [dot_nn(dscores[h], keys[h]) * (scales[h] * SCALE) for h in every]
            stats = jnp.zeros((BLOCK, BLOCK), F32)
            for h in every:
                stats = jnp.where(lane == h, peaks[h] + jnp.log2(totals[h]), stats)
                stats = jnp.where(lane == heads + h, deltas[h], stats)
            for h in every:
                out_ref[i, 0, :, head_of(h)] = outs[h].astype(BF16)
                out_ref[i, 1, :, head_of(h)] = grads[h].astype(BF16)
            stat_ref[i] = stats.T[: 2 * heads]

        by_width(cross_ref[i], width, body)
        return 0

    lax.fori_loop(0, qg_ref.shape[0], block, 0)


def key_kernel(
    width, heads, slot_ref, valid_ref, place_ref, cross_ref, count_ref, kv_ref, stat_ref, qg_local,
    below, above, extra, out_ref, pool, sem, extra_sem,
):
    fill_pool(count_ref[0], (qg_local, below, above), pool, extra, sem, extra_sem)

    def block(j, _):
        def body(count):
            slots = [slot_ref[j, t] for t in range(count)]
            places = [place_ref[j, t] for t in range(count)]

            def log_tile(t, h):
                row = stat_ref[places[t], pl.ds(h, 1), :]
                return jnp.where(valid_ref[j, t] > 0, row, POS) if unsure(t) else row

            every = range(heads)
            queries = [jnp.concatenate([pool[s, 0, :, head_of(h)] for s in slots], axis=0) for h in every]
            upstream = [jnp.concatenate([pool[s, 1, :, head_of(h)] for s in slots], axis=0) for h in every]
            logs = [jnp.concatenate([log_tile(t, h) for t in range(count)], axis=1) for h in every]
            deltas = [
                jnp.concatenate([stat_ref[p, pl.ds(heads + h, 1), :] for p in places], axis=1)
                for h in every
            ]
            scores = [dot_nt(kv_ref[j, 0, :, head_of(h)], queries[h]) for h in every]
            dprobs = [dot_nt(kv_ref[j, 1, :, head_of(h)], upstream[h]) for h in every]
            probs = [jnp.exp2(scores[h] * SCALE2 - logs[h]) for h in every]
            dscores = [(probs[h] * (dprobs[h] - deltas[h])).astype(BF16) for h in every]
            grad_v = [dot_nn(probs[h].astype(BF16), upstream[h]) for h in every]
            grad_k = [dot_nn(dscores[h], queries[h]) * SCALE for h in every]
            for h in every:
                out_ref[j, 1, :, head_of(h)] = grad_v[h].astype(BF16)
                out_ref[j, 0, :, head_of(h)] = grad_k[h].astype(BF16)

        by_width(cross_ref[j], width, body)
        return 0

    lax.fori_loop(0, kv_ref.shape[0], block, 0)


def patterns_of(steps):
    groups, index = [], {}
    for d in range(1, steps):
        top = 1 << (d.bit_length() - 1)
        for low in range(top):
            pairs = [a for a in range(steps) if not a & top and a % top == low]
            for a in pairs:
                index[a, a ^ d] = index[a ^ d, a] = len(groups)
            groups.append([(a, a ^ d) for a in pairs] + [(a ^ d, a) for a in pairs])
    return groups, index


def tables(block_mask, spans, span_len, steps, groups):
    z = lax.axis_index("z")
    local = spans * SUB
    most = (spans * (spans - 1) + len(groups)) // 2
    capacity = 2 * most
    iota = functools.partial(lax.broadcasted_iota, jnp.int32)
    as_int = lambda flags: flags.astype(jnp.int32)
    cube = block_mask.reshape(spans, span_len, spans, span_len)
    partner = jnp.sum(cube * (iota(cube.shape, 3) + 1), axis=3) - 1
    shape = partner.shape
    mine, spot, other = iota(shape, 0), iota(shape, 1), iota(shape, 2)
    linked = (partner >= 0) & (mine != other)
    here, there = spot // SUB, partner // SUB
    hop = jnp.where(linked, here ^ there, 0)
    top = sum(as_int(hop >= (1 << n)) << n for n in range(steps.bit_length()))
    top = (top + 1) // 2
    low = jnp.minimum(here, there) & (jnp.maximum(top, 1) - 1)
    group = jnp.where(hop > 0, base_of(hop, top) + low, -1)
    per_place = group.reshape(spans, steps, SUB, spans)
    numbers = iota((len(groups), spans, steps, SUB, spans), 0)
    rounds = (jnp.max(jnp.sum(as_int(per_place[None] == numbers), axis=(1, 3, 4)), axis=1) + 1) // 2
    number = iota((len(groups), len(groups)), 0)
    ends = jnp.sum(jnp.where(number <= iota(number.shape, 1), rounds[:, None], 0), axis=0)
    starts = ends - rounds
    total = jnp.sum(rounds)
    at = iota((most, len(groups)), 0)
    plan = jnp.minimum(jnp.sum(as_int(at >= ends[None]), axis=1), len(groups) - 1)
    key = jnp.where(
        mine < other,
        (mine * span_len + spot) * spans + other,
        (other * span_len + partner) * spans + mine,
    )

    def at_place(table):
        return lax.dynamic_slice_in_dim(table, z * SUB, SUB, 1).reshape(local, spans)

    partner_l, linked_l, group_l, key_l = [at_place(t) for t in (partner, linked, group, key)]
    other_l = iota((local, spans), 1)
    block_l = iota((local, spans), 0)
    order = (group_l * (spans * span_len * spans) + key_l).reshape(-1)
    flat = group_l.reshape(-1)
    crossing = flat >= 0
    same = crossing[None, :] & (flat[None, :] == flat[:, None])
    rank = jnp.sum(as_int(same & (order[None, :] < order[:, None])), axis=1)
    first = jnp.sum(
        jnp.where(flat[:, None] == iota((local * spans, len(groups)), 1), starts[None], 0), axis=1
    )
    extra_slot = 2 * first + rank
    hits = crossing[:, None] & (extra_slot[:, None] == iota((local * spans, capacity), 1))
    send_block = jnp.sum(as_int(hits) * block_l.reshape(-1)[:, None], axis=0).reshape(most, 2)
    plan = (plan * local + send_block[:, 0]) * local + send_block[:, 1]
    cross_slot = jnp.where(
        group_l >= 0,
        local + 2 * spans + extra_slot.reshape(local, spans),
        other_l * SUB + partner_l % SUB,
    )
    cross_place = (z ^ (partner_l // SUB)) * local + other_l * SUB + partner_l % SUB
    own = block_l[:, :1]
    span_l, x_l = own // SUB, own % SUB
    pair = own + 1 - 2 * x_l
    near_slot = jnp.where(x_l == 0, local + span_l, local + spans + span_l)
    near_ok = jnp.where(x_l == 0, z > 0, z < steps - 1)
    near_place = jnp.where(x_l == 0, (z ^ (z - 1)) * local + own + 1, (z ^ (z + 1)) * local + own - 1)
    before = iota((local, spans, spans), 2) < iota((local, spans, spans), 1)
    position = jnp.sum(as_int(linked_l[:, None, :] & before), axis=2)
    chosen = linked_l[:, None, :] & (position[:, None, :] == iota((local, spans - 1, spans), 1))

    def pick(table):
        return jnp.sum(jnp.where(chosen, table[:, None, :], 0), axis=2)

    sure = jnp.ones_like(own)
    ok = jnp.concatenate([sure, sure, as_int(near_ok), pick(as_int(linked_l))], axis=1)
    slot = jnp.concatenate([own, pair, near_slot, pick(cross_slot)], axis=1)
    place = jnp.concatenate([own, pair, near_place, pick(cross_place)], axis=1)
    slot = jnp.where(ok > 0, slot, own)
    place = jnp.where(ok > 0, place, own)
    cross = jnp.sum(as_int(linked_l), axis=1)
    return slot, ok, place, cross, total, plan, capacity


def base_of(hop, top):
    smaller = (top * top - 1) // 3
    return smaller + (hop - top) * top


def shards(query_tokens, key_tokens, value_tokens, cotangent, block_mask):
    spans = lax.axis_size("blk")
    steps = lax.axis_size("z")
    span_len = steps * SUB
    local = spans * SUB
    groups, _ = patterns_of(steps)

    def exchange(pair):
        return lax.all_to_all(pair, ("blk", "x"), split_axis=0, concat_axis=0, tiled=True)

    kv = exchange(pack(key_tokens, value_tokens, local))
    qg = exchange(pack(query_tokens, cotangent, local))
    columns = kv.shape[3]
    heads = columns // HEAD_DIM
    slot, ok, place, cross, total, plan, capacity = tables(
        block_mask, spans, span_len, steps, groups
    )
    width = slot.shape[1]
    upward = [(n, n + 1) for n in range(steps - 1)]
    downward = [(n + 1, n) for n in range(steps - 1)]

    def neighbours(pair):
        edges = pair.reshape(spans, SUB, 2, BLOCK, columns)
        below = lax.ppermute(edges[:, SUB - 1], "z", upward)
        above = lax.ppermute(edges[:, 0], "z", downward)
        return below, above

    kv_below, kv_above = neighbours(kv)
    qg_below, qg_above = neighbours(qg)

    def crossing(pair):
        buffer = pl.pallas_call(
            lambda out_ref: None,
            out_shape=jax.ShapeDtypeStruct((capacity, 2, BLOCK, columns), BF16),
            out_specs=pl.BlockSpec(memory_space=pl.ANY),
            name="extra_blocks",
        )()
        swaps = [functools.partial(lax.ppermute, axis_name="z", perm=g) for g in groups]

        def one_round(r, held):
            code = plan[r]
            first, second = code // local % local, code % local
            sent = jnp.concatenate(
                [lax.dynamic_slice_in_dim(pair, n, 1, 0) for n in (first, second)]
            )
            got = lax.switch(code // (local * local), swaps, sent)
            return lax.dynamic_update_slice_in_dim(held, got, 2 * r, 0)

        return lax.fori_loop(0, total, one_round, buffer)

    kv_extra = crossing(kv)
    qg_extra = crossing(qg)
    count = 2 * total.reshape(1)

    smem = pl.BlockSpec(memory_space=pltpu.SMEM)
    vmem = pl.BlockSpec(memory_space=pltpu.VMEM)
    anywhere = pl.BlockSpec(memory_space=pl.ANY)
    scratch = [
        pltpu.VMEM((local + 2 * spans + capacity, 2, BLOCK, columns), BF16),
        pltpu.SemaphoreType.DMA((3,)),
        pltpu.SemaphoreType.DMA((capacity,)),
    ]
    cost = pl.CostEstimate(
        flops=2 * 4 * local * heads * width * BLOCK * BLOCK * HEAD_DIM,
        bytes_accessed=16 * local * BLOCK * columns,
        transcendentals=local * heads * width * BLOCK * BLOCK,
    )
    out_pair, stats = pl.pallas_call(
        functools.partial(query_kernel, width, heads),
        out_shape=(
            jax.ShapeDtypeStruct(qg.shape, BF16),
            jax.ShapeDtypeStruct((local, 2 * heads, BLOCK), F32),
        ),
        in_specs=[smem] * 4 + [vmem] + [anywhere] * 4,
        out_specs=(vmem, vmem),
        scratch_shapes=scratch,
        cost_estimate=cost,
        name="query_pass",
    )(slot, ok, cross, count, qg, kv, kv_below, kv_above, kv_extra)
    far = [lax.ppermute(stats, "z", [(n, n ^ d) for n in range(steps)]) for d in range(1, steps)]
    all_stats = jnp.concatenate([stats] + far)
    grad_pair = pl.pallas_call(
        functools.partial(key_kernel, width, heads),
        out_shape=jax.ShapeDtypeStruct(kv.shape, BF16),
        in_specs=[smem] * 5 + [vmem, vmem] + [anywhere] * 4,
        out_specs=vmem,
        scratch_shapes=scratch,
        cost_estimate=cost,
        name="key_pass",
    )(slot, ok, place, cross, count, kv, all_stats, qg, qg_below, qg_above, qg_extra)
    out_back = exchange(out_pair)
    grad_back = exchange(grad_pair)
    attended, grad_query = unpack(out_back)
    grad_key, grad_value = unpack(grad_back)
    return attended, grad_query, grad_key, grad_value


def solution(mesh):
    spans, ulysses = mesh.shape["blk"], mesh.shape["ulysses"]
    split = Mesh(mesh.devices.reshape(spans, ulysses // SUB, SUB), ("blk", "z", "x"))
    tokens = P(("blk", "z", "x"), None)
    return jax.shard_map(
        shards,
        mesh=split,
        in_specs=(tokens, tokens, tokens, tokens, P()),
        out_specs=(tokens, tokens, tokens, tokens),
        check_vma=False,
    )
```

```python
import functools
import math
import jax
import jax.numpy as jnp
from jax import lax
from jax.experimental import pallas as pl
from jax.experimental.pallas import tpu as pltpu
from jax.sharding import Mesh, PartitionSpec as P

HEAD_DIM = 128
BLOCK = 128
SUB = 2
NEG = float("-inf")
POS = float("inf")
BF16 = jnp.bfloat16
F32 = jnp.float32
SCALE = HEAD_DIM ** (-0.5)
SCALE2 = SCALE * math.log2(math.e)
OWN = 3
WIDE = 4


def head_of(h):
    return slice(h * HEAD_DIM, (h + 1) * HEAD_DIM)


def dot_nt(a, b):
    return lax.dot_general(a, b, (((1,), (1,)), ((), ())), preferred_element_type=F32)


def dot_nn(a, b):
    return lax.dot_general(a, b, (((1,), (0,)), ((), ())), preferred_element_type=F32)


def pack_kernel(a_ref, b_ref, out_ref, held, in_sem, out_sem):
    groups, _, _, columns = out_ref.shape
    arrive, leave = [], []
    for c in range(groups):
        for n, source in enumerate((a_ref, b_ref)):
            arrive.append(
                pltpu.make_async_copy(
                    source.at[:, c * columns : (c + 1) * columns], held.at[c, n], in_sem.at[c, n]
                )
            )
            leave.append(pltpu.make_async_copy(held.at[c, n], out_ref.at[c, n], out_sem.at[c, n]))
    for copy in arrive:
        copy.start()
    for first, second in zip(arrive, leave):
        first.wait()
        second.start()
    for copy in leave:
        copy.wait()


def unpack_kernel(in_ref, a_ref, b_ref, sem):
    groups, _, _, columns = in_ref.shape
    copies = [
        pltpu.make_async_copy(
            in_ref.at[c, n], target.at[:, c * columns : (c + 1) * columns], sem.at[c, n]
        )
        for c in range(groups)
        for n, target in enumerate((a_ref, b_ref))
    ]
    for copy in copies:
        copy.start()
    for copy in copies:
        copy.wait()


def pack(a, b, groups):
    rows, columns = a.shape
    shape = (groups, 2, rows, columns // groups)
    anywhere = pl.BlockSpec(memory_space=pl.ANY)
    return pl.pallas_call(
        pack_kernel,
        out_shape=jax.ShapeDtypeStruct(shape, a.dtype),
        in_specs=[anywhere] * 2,
        out_specs=anywhere,
        scratch_shapes=[
            pltpu.VMEM(shape, a.dtype),
            pltpu.SemaphoreType.DMA((groups, 2)),
            pltpu.SemaphoreType.DMA((groups, 2)),
        ],
        name="pack",
    )(a, b)


def unpack(pair):
    groups, _, rows, columns = pair.shape
    anywhere = pl.BlockSpec(memory_space=pl.ANY)
    flat = jax.ShapeDtypeStruct((rows, groups * columns), pair.dtype)
    return pl.pallas_call(
        unpack_kernel,
        out_shape=(flat, flat),
        in_specs=[pl.BlockSpec(memory_space=pltpu.VMEM)],
        out_specs=(anywhere, anywhere),
        scratch_shapes=[pltpu.SemaphoreType.DMA((groups, 2))],
        compiler_params=pltpu.CompilerParams(vmem_limit_bytes=5 * rows * groups * columns),
        name="unpack",
    )(pair)


def fill_pool(count, parts, pool, extra, sem, extra_sem):
    copies = []
    start = 0
    for m, source in enumerate(parts):
        size = source.shape[0]
        copies.append(pltpu.make_async_copy(source, pool.at[pl.ds(start, size)], sem.at[m]))
        start += size
    for copy in copies:
        copy.start()

    ahead, rest = extra
    early = ahead.shape[0]

    def move(slot):
        return pltpu.make_async_copy(rest.at[slot - early], pool.at[start + slot], extra_sem.at[slot])

    def move_ahead():
        return pltpu.make_async_copy(ahead, pool.at[pl.ds(start, early)], extra_sem.at[0])

    @pl.when(count > 0)
    def _():
        move_ahead().start()

    lax.fori_loop(early, count, lambda slot, _: (move(slot).start(), 0)[1], 0)
    for copy in copies:
        copy.wait()

    @pl.when(count > 0)
    def _():
        move_ahead().wait()

    lax.fori_loop(early, count, lambda slot, _: (move(slot).wait(), 0)[1], 0)


def by_width(cross, width, body):
    top = min(OWN, width - OWN)
    for n in range(top):

        @pl.when(cross == n)
        def _(n=n):
            body(OWN + n)

    @pl.when(cross >= top)
    def _():
        body(width)


def unsure(t):
    return t == OWN - 1 or t >= 2 * OWN


def query_kernel(
    width, heads, slot_ref, valid_ref, cross_ref, count_ref, qg_ref, kv_local, below, above, ahead, rest,
    out_ref, stat_ref, pool, sem, extra_sem,
):
    fill_pool(count_ref[0], (kv_local, below, above), pool, (ahead, rest), sem, extra_sem)
    lane = lax.broadcasted_iota(jnp.int32, (BLOCK, BLOCK), 1)

    def block(i, _):
        def body(count):
            slots = [slot_ref[i, t] for t in range(count)]
            bias = jnp.concatenate(
                [
                    jnp.full((1, BLOCK), jnp.where(valid_ref[i, t] > 0, 0.0, NEG), F32)
                    if unsure(t)
                    else jnp.zeros((1, BLOCK), F32)
                    for t in range(count)
                ],
                axis=1,
            )
            every = range(heads)
            keys = [jnp.concatenate([pool[s, 0, :, head_of(h)] for s in slots], axis=0) for h in every]
            values = [jnp.concatenate([pool[s, 1, :, head_of(h)] for s in slots], axis=0) for h in every]
            upstream = [qg_ref[i, 1, :, head_of(h)] for h in every]
            scores = [dot_nt(qg_ref[i, 0, :, head_of(h)], keys[h]) * SCALE2 + bias for h in every]
            dprobs = [dot_nt(upstream[h], values[h]) for h in every]
            peaks = [jnp.max(scores[h], axis=1, keepdims=True) for h in every]
            probs = [jnp.exp2(scores[h] - peaks[h]) for h in every]
            totals = [jnp.sum(probs[h], axis=1, keepdims=True) for h in every]
            scales = [1.0 / totals[h] for h in every]
            outs = [dot_nn(probs[h].astype(BF16), values[h]) * scales[h] for h in every]
            deltas = [
                jnp.sum(upstream[h].astype(F32) * outs[h], axis=1, keepdims=True) for h in every
            ]
            dscores = [(probs[h] * (dprobs[h] - deltas[h])).astype(BF16) for h in every]
            grads = [dot_nn(dscores[h], keys[h]) * (scales[h] * SCALE) for h in every]
            stats = jnp.zeros((BLOCK, BLOCK), F32)
            for h in every:
                stats = jnp.where(lane == h, peaks[h] + jnp.log2(totals[h]), stats)
                stats = jnp.where(lane == heads + h, deltas[h], stats)
            for h in every:
                out_ref[i, 0, :, head_of(h)] = outs[h].astype(BF16)
                out_ref[i, 1, :, head_of(h)] = grads[h].astype(BF16)
            stat_ref[i] = stats.T[: 2 * heads]

        by_width(cross_ref[i], width, body)
        return 0

    lax.fori_loop(0, qg_ref.shape[0], block, 0)


def key_kernel(
    width, heads, slot_ref, valid_ref, place_ref, cross_ref, count_ref, kv_ref, stat_ref, qg_local,
    below, above, ahead, rest, out_ref, pool, sem, extra_sem,
):
    fill_pool(count_ref[0], (qg_local, below, above), pool, (ahead, rest), sem, extra_sem)

    def block(j, _):
        def body(count):
            slots = [slot_ref[j, t] for t in range(count)]
            places = [place_ref[j, t] for t in range(count)]

            def log_tile(t, h):
                row = stat_ref[places[t], pl.ds(h, 1), :]
                return jnp.where(valid_ref[j, t] > 0, row, POS) if unsure(t) else row

            every = range(heads)
            queries = [jnp.concatenate([pool[s, 0, :, head_of(h)] for s in slots], axis=0) for h in every]
            upstream = [jnp.concatenate([pool[s, 1, :, head_of(h)] for s in slots], axis=0) for h in every]
            logs = [jnp.concatenate([log_tile(t, h) for t in range(count)], axis=1) for h in every]
            deltas = [
                jnp.concatenate([stat_ref[p, pl.ds(heads + h, 1), :] for p in places], axis=1)
                for h in every
            ]
            scores = [dot_nt(kv_ref[j, 0, :, head_of(h)], queries[h]) for h in every]
            dprobs = [dot_nt(kv_ref[j, 1, :, head_of(h)], upstream[h]) for h in every]
            probs = [jnp.exp2(scores[h] * SCALE2 - logs[h]) for h in every]
            dscores = [(probs[h] * (dprobs[h] - deltas[h])).astype(BF16) for h in every]
            grad_v = [dot_nn(probs[h].astype(BF16), upstream[h]) for h in every]
            grad_k = [dot_nn(dscores[h], queries[h]) * SCALE for h in every]
            for h in every:
                out_ref[j, 1, :, head_of(h)] = grad_v[h].astype(BF16)
                out_ref[j, 0, :, head_of(h)] = grad_k[h].astype(BF16)

        by_width(cross_ref[j], width, body)
        return 0

    lax.fori_loop(0, kv_ref.shape[0], block, 0)


def patterns_of(steps):
    groups, index = [], {}
    for d in range(1, steps):
        top = 1 << (d.bit_length() - 1)
        for low in range(top):
            pairs = [a for a in range(steps) if not a & top and a % top == low]
            for a in pairs:
                index[a, a ^ d] = index[a ^ d, a] = len(groups)
            groups.append([(a, a ^ d) for a in pairs] + [(a ^ d, a) for a in pairs])
    return groups, index


def tables(block_mask, spans, span_len, steps, groups):
    z = lax.axis_index("z")
    local = spans * SUB
    most = (spans * (spans - 1) + (WIDE - 1) * len(groups)) // WIDE
    capacity = WIDE * most
    iota = functools.partial(lax.broadcasted_iota, jnp.int32)
    as_int = lambda flags: flags.astype(jnp.int32)
    cube = block_mask.reshape(spans, span_len, spans, span_len)
    partner = jnp.sum(cube * (iota(cube.shape, 3) + 1), axis=3) - 1
    shape = partner.shape
    mine, spot, other = iota(shape, 0), iota(shape, 1), iota(shape, 2)
    linked = (partner >= 0) & (mine != other)
    here, there = spot // SUB, partner // SUB
    hop = jnp.where(linked, here ^ there, 0)
    top = sum(as_int(hop >= (1 << n)) << n for n in range(steps.bit_length()))
    top = (top + 1) // 2
    low = jnp.minimum(here, there) & (jnp.maximum(top, 1) - 1)
    group = jnp.where(hop > 0, base_of(hop, top) + low, -1)
    per_place = group.reshape(spans, steps, SUB, spans)
    numbers = iota((len(groups), spans, steps, SUB, spans), 0)
    messages = jnp.max(jnp.sum(as_int(per_place[None] == numbers), axis=(1, 3, 4)), axis=1)
    rounds = (messages + WIDE - 1) // WIDE
    number = iota((len(groups), len(groups)), 0)
    ends = jnp.sum(jnp.where(number <= iota(number.shape, 1), rounds[:, None], 0), axis=0)
    starts = ends - rounds
    total = jnp.sum(rounds)
    at = iota((most, len(groups)), 0)
    plan = jnp.minimum(jnp.sum(as_int(at >= ends[None]), axis=1), len(groups) - 1)
    left = jnp.sum(
        jnp.where(plan[:, None] == iota(at.shape, 1), messages[None] - WIDE * (at - starts[None]), 0), axis=1
    )
    plan = 2 * plan + as_int(left <= WIDE // 2)
    key = jnp.where(
        mine < other,
        (mine * span_len + spot) * spans + other,
        (other * span_len + partner) * spans + mine,
    )

    def at_place(table):
        return lax.dynamic_slice_in_dim(table, z * SUB, SUB, 1).reshape(local, spans)

    partner_l, linked_l, group_l, key_l = [at_place(t) for t in (partner, linked, group, key)]
    other_l = iota((local, spans), 1)
    block_l = iota((local, spans), 0)
    order = (group_l * (spans * span_len * spans) + key_l).reshape(-1)
    flat = group_l.reshape(-1)
    crossing = flat >= 0
    same = crossing[None, :] & (flat[None, :] == flat[:, None])
    rank = jnp.sum(as_int(same & (order[None, :] < order[:, None])), axis=1)
    first = jnp.sum(
        jnp.where(flat[:, None] == iota((local * spans, len(groups)), 1), starts[None], 0), axis=1
    )
    extra_slot = WIDE * first + rank
    hits = crossing[:, None] & (extra_slot[:, None] == iota((local * spans, capacity), 1))
    send_block = jnp.sum(as_int(hits) * block_l.reshape(-1)[:, None], axis=0).reshape(most, WIDE)
    for n in range(WIDE):
        plan = plan * local + send_block[:, n]
    cross_slot = jnp.where(
        group_l >= 0,
        local + 2 * spans + extra_slot.reshape(local, spans),
        other_l * SUB + partner_l % SUB,
    )
    cross_place = (z ^ (partner_l // SUB)) * local + other_l * SUB + partner_l % SUB
    own = block_l[:, :1]
    span_l, x_l = own // SUB, own % SUB
    pair = own + 1 - 2 * x_l
    near_slot = jnp.where(x_l == 0, local + span_l, local + spans + span_l)
    near_ok = jnp.where(x_l == 0, z > 0, z < steps - 1)
    near_place = jnp.where(x_l == 0, (z ^ (z - 1)) * local + own + 1, (z ^ (z + 1)) * local + own - 1)
    before = iota((local, spans, spans), 2) < iota((local, spans, spans), 1)
    position = jnp.sum(as_int(linked_l[:, None, :] & before), axis=2)
    chosen = linked_l[:, None, :] & (position[:, None, :] == iota((local, spans - 1, spans), 1))

    def pick(table):
        return jnp.sum(jnp.where(chosen, table[:, None, :], 0), axis=2)

    sure = jnp.ones_like(own)
    ok = jnp.concatenate([sure, sure, as_int(near_ok), pick(as_int(linked_l))], axis=1)
    slot = jnp.concatenate([own, pair, near_slot, pick(cross_slot)], axis=1)
    place = jnp.concatenate([own, pair, near_place, pick(cross_place)], axis=1)
    slot = jnp.where(ok > 0, slot, own)
    place = jnp.where(ok > 0, place, own)
    cross = jnp.sum(as_int(linked_l), axis=1)
    return slot, ok, place, cross, total, plan, capacity


def base_of(hop, top):
    smaller = (top * top - 1) // 3
    return smaller + (hop - top) * top


def shards(query_tokens, key_tokens, value_tokens, cotangent, block_mask):
    spans = lax.axis_size("blk")
    steps = lax.axis_size("z")
    span_len = steps * SUB
    local = spans * SUB
    groups, _ = patterns_of(steps)

    def exchange(pair):
        return lax.all_to_all(pair, ("blk", "x"), split_axis=0, concat_axis=0, tiled=True)

    kv = exchange(pack(key_tokens, value_tokens, local))
    qg = exchange(pack(query_tokens, cotangent, local))
    columns = kv.shape[3]
    heads = columns // HEAD_DIM
    slot, ok, place, cross, total, plan, capacity = tables(
        block_mask, spans, span_len, steps, groups
    )
    width = slot.shape[1]
    upward = [(n, n + 1) for n in range(steps - 1)]
    downward = [(n + 1, n) for n in range(steps - 1)]

    def neighbours(pair):
        edges = pair.reshape(spans, SUB, 2, BLOCK, columns)
        below = lax.ppermute(edges[:, SUB - 1], "z", upward)
        above = lax.ppermute(edges[:, 0], "z", downward)
        return below, above

    kv_below, kv_above = neighbours(kv)
    qg_below, qg_above = neighbours(qg)

    def take(code):
        picks = []
        for _ in range(WIDE):
            picks.insert(0, code % local)
            code = code // local
        return code, picks

    def swap(pair, *picks, group, size):
        sent = jnp.concatenate([lax.dynamic_slice_in_dim(pair, n, 1, 0) for n in picks[:size]])
        got = lax.ppermute(sent, "z", group)
        return jnp.concatenate([got] * (WIDE // size))

    swaps = [
        lambda pair, *picks, g=g, n=n: swap(pair, *picks, group=g, size=n)
        for g in groups
        for n in (WIDE, WIDE // 2)
    ]
    blank = functools.partial(
        pl.pallas_call,
        lambda out_ref: None,
        out_specs=pl.BlockSpec(memory_space=pl.ANY),
        compiler_params=pltpu.CompilerParams(vmem_limit_bytes=1 << 20),
        name="extra_blocks",
    )

    def crossing(pair):
        size = (WIDE, 2, BLOCK, columns)
        unused = blank(out_shape=jax.ShapeDtypeStruct(size, BF16))()
        buffer = blank(out_shape=jax.ShapeDtypeStruct((capacity - WIDE,) + size[1:], BF16))()

        def one_round(r, held):
            code, picks = take(plan[r])
            got = lax.switch(code // 2, swaps[::2], pair, *picks)
            return lax.dynamic_update_slice_in_dim(held, got, WIDE * (r - 1), 0)

        code, picks = take(plan[0])
        skip = [lambda held, pair, *picks: held]
        some = [lambda held, pair, *picks, f=f: f(pair, *picks) for f in swaps]
        ahead = lax.switch(
            jnp.where(total > 0, code + 1, 0), skip + some, unused, pair, *picks
        )
        return ahead, lax.fori_loop(1, total, one_round, buffer)

    kv_extra = crossing(kv)
    count = WIDE * total.reshape(1)

    smem = pl.BlockSpec(memory_space=pltpu.SMEM)
    vmem = pl.BlockSpec(memory_space=pltpu.VMEM)
    anywhere = pl.BlockSpec(memory_space=pl.ANY)
    scratch = [
        pltpu.VMEM((local + 2 * spans + capacity, 2, BLOCK, columns), BF16),
        pltpu.SemaphoreType.DMA((3,)),
        pltpu.SemaphoreType.DMA((capacity,)),
    ]
    block_bytes = 2 * 2 * BLOCK * columns
    grant = block_bytes * (capacity + 2 * spans + 6 * local) + (10 << 20)
    cost = pl.CostEstimate(
        flops=2 * 4 * local * heads * width * BLOCK * BLOCK * HEAD_DIM,
        bytes_accessed=16 * local * BLOCK * columns,
        transcendentals=local * heads * width * BLOCK * BLOCK,
    )
    out_pair, stats = pl.pallas_call(
        functools.partial(query_kernel, width, heads),
        out_shape=(
            jax.ShapeDtypeStruct(qg.shape, BF16),
            jax.ShapeDtypeStruct((local, 2 * heads, BLOCK), F32),
        ),
        in_specs=[smem] * 4 + [vmem] + [anywhere] * 5,
        out_specs=(vmem, vmem),
        scratch_shapes=scratch,
        cost_estimate=cost,
        compiler_params=pltpu.CompilerParams(vmem_limit_bytes=grant),
        name="query_pass",
    )(slot, ok, cross, count, qg, kv, kv_below, kv_above, *kv_extra)
    far = [lax.ppermute(stats, "z", [(n, n ^ d) for n in range(steps)]) for d in range(1, steps)]
    all_stats = jnp.concatenate([stats] + far)
    qg_late, all_stats = lax.optimization_barrier((qg, all_stats))
    qg_extra = crossing(qg_late)
    grad_pair = pl.pallas_call(
        functools.partial(key_kernel, width, heads),
        out_shape=jax.ShapeDtypeStruct(kv.shape, BF16),
        in_specs=[smem] * 5 + [vmem, vmem] + [anywhere] * 5,
        out_specs=vmem,
        scratch_shapes=scratch,
        cost_estimate=cost,
        compiler_params=pltpu.CompilerParams(vmem_limit_bytes=grant),
        name="key_pass",
    )(slot, ok, place, cross, count, kv, all_stats, qg, qg_below, qg_above, *qg_extra)
    out_back = exchange(out_pair)
    grad_back = exchange(grad_pair)
    attended, grad_query = unpack(out_back)
    grad_key, grad_value = unpack(grad_back)
    return attended, grad_query, grad_key, grad_value


def solution(mesh):
    spans, ulysses = mesh.shape["blk"], mesh.shape["ulysses"]
    split = Mesh(mesh.devices.reshape(spans, ulysses // SUB, SUB), ("blk", "z", "x"))
    tokens = P(("blk", "z", "x"), None)
    return jax.shard_map(
        shards,
        mesh=split,
        in_specs=(tokens, tokens, tokens, tokens, P()),
        out_specs=(tokens, tokens, tokens, tokens),
        check_vma=False,
    )
```

```python
import functools
import math
import jax
import jax.numpy as jnp
from jax import lax
from jax.experimental import pallas as pl
from jax.experimental.pallas import tpu as pltpu
from jax.sharding import Mesh, PartitionSpec as P

HEAD_DIM = 128
BLOCK = 128
SUB = 2
NEG = float("-inf")
POS = float("inf")
BF16 = jnp.bfloat16
F32 = jnp.float32
SCALE = HEAD_DIM ** (-0.5)
SCALE2 = SCALE * math.log2(math.e)
OWN = 3
WIDE = 4


def head_of(h):
    return slice(h * HEAD_DIM, (h + 1) * HEAD_DIM)


def dot_nt(a, b):
    return lax.dot_general(a, b, (((1,), (1,)), ((), ())), preferred_element_type=F32)


def dot_nn(a, b):
    return lax.dot_general(a, b, (((1,), (0,)), ((), ())), preferred_element_type=F32)


def pack_kernel(a_ref, b_ref, out_ref, held, in_sem, out_sem):
    groups, _, _, columns = out_ref.shape
    arrive, leave = [], []
    for c in range(groups):
        for n, source in enumerate((a_ref, b_ref)):
            arrive.append(
                pltpu.make_async_copy(
                    source.at[:, c * columns : (c + 1) * columns], held.at[c, n], in_sem.at[c, n]
                )
            )
            leave.append(pltpu.make_async_copy(held.at[c, n], out_ref.at[c, n], out_sem.at[c, n]))
    for copy in arrive:
        copy.start()
    for first, second in zip(arrive, leave):
        first.wait()
        second.start()
    for copy in leave:
        copy.wait()


def unpack_kernel(in_ref, a_ref, b_ref, sem):
    groups, _, _, columns = in_ref.shape
    copies = [
        pltpu.make_async_copy(
            in_ref.at[c, n], target.at[:, c * columns : (c + 1) * columns], sem.at[c, n]
        )
        for c in range(groups)
        for n, target in enumerate((a_ref, b_ref))
    ]
    for copy in copies:
        copy.start()
    for copy in copies:
        copy.wait()


def pack(a, b, groups):
    rows, columns = a.shape
    shape = (groups, 2, rows, columns // groups)
    anywhere = pl.BlockSpec(memory_space=pl.ANY)
    return pl.pallas_call(
        pack_kernel,
        out_shape=jax.ShapeDtypeStruct(shape, a.dtype),
        in_specs=[anywhere] * 2,
        out_specs=anywhere,
        scratch_shapes=[
            pltpu.VMEM(shape, a.dtype),
            pltpu.SemaphoreType.DMA((groups, 2)),
            pltpu.SemaphoreType.DMA((groups, 2)),
        ],
        name="pack",
    )(a, b)


def unpack(pair):
    groups, _, rows, columns = pair.shape
    anywhere = pl.BlockSpec(memory_space=pl.ANY)
    flat = jax.ShapeDtypeStruct((rows, groups * columns), pair.dtype)
    return pl.pallas_call(
        unpack_kernel,
        out_shape=(flat, flat),
        in_specs=[pl.BlockSpec(memory_space=pltpu.VMEM)],
        out_specs=(anywhere, anywhere),
        scratch_shapes=[pltpu.SemaphoreType.DMA((groups, 2))],
        compiler_params=pltpu.CompilerParams(vmem_limit_bytes=5 * rows * groups * columns),
        name="unpack",
    )(pair)


def fill_pool(count, parts, pool, extra, sem, extra_sem):
    copies = []
    start = 0
    for m, source in enumerate(parts):
        size = source.shape[0]
        copies.append(pltpu.make_async_copy(source, pool.at[pl.ds(start, size)], sem.at[m]))
        start += size
    for copy in copies:
        copy.start()

    ahead, rest = extra
    early = ahead.shape[0]

    def move(slot):
        return pltpu.make_async_copy(rest.at[slot - early], pool.at[start + slot], extra_sem.at[slot])

    def move_ahead():
        return pltpu.make_async_copy(ahead, pool.at[pl.ds(start, early)], extra_sem.at[0])

    @pl.when(count > 0)
    def _():
        move_ahead().start()

    lax.fori_loop(early, count, lambda slot, _: (move(slot).start(), 0)[1], 0)
    for copy in copies:
        copy.wait()

    @pl.when(count > 0)
    def _():
        move_ahead().wait()

    lax.fori_loop(early, count, lambda slot, _: (move(slot).wait(), 0)[1], 0)


def by_width(cross, width, body):
    top = min(OWN, width - OWN)
    for n in range(top):

        @pl.when(cross == n)
        def _(n=n):
            body(OWN + n)

    @pl.when(cross >= top)
    def _():
        body(width)


def unsure(t):
    return t == OWN - 1 or t >= 2 * OWN


def query_kernel(
    width, heads, slot_ref, valid_ref, cross_ref, count_ref, qg_ref, kv_local, below, above, ahead, rest,
    out_ref, stat_ref, pool, sem, extra_sem,
):
    fill_pool(count_ref[0], (kv_local, below, above), pool, (ahead, rest), sem, extra_sem)
    lane = lax.broadcasted_iota(jnp.int32, (BLOCK, BLOCK), 1)

    def block(i, _):
        def body(count):
            slots = [slot_ref[i, t] for t in range(count)]
            bias = jnp.concatenate(
                [
                    jnp.full((1, BLOCK), jnp.where(valid_ref[i, t] > 0, 0.0, NEG), F32)
                    if unsure(t)
                    else jnp.zeros((1, BLOCK), F32)
                    for t in range(count)
                ],
                axis=1,
            )
            every = range(heads)
            keys = [jnp.concatenate([pool[s, 0, :, head_of(h)] for s in slots], axis=0) for h in every]
            values = [jnp.concatenate([pool[s, 1, :, head_of(h)] for s in slots], axis=0) for h in every]
            upstream = [qg_ref[i, 1, :, head_of(h)] for h in every]
            scores = [dot_nt(qg_ref[i, 0, :, head_of(h)], keys[h]) * SCALE2 + bias for h in every]
            dprobs = [dot_nt(upstream[h], values[h]) for h in every]
            peaks = [jnp.max(scores[h], axis=1, keepdims=True) for h in every]
            probs = [jnp.exp2(scores[h] - peaks[h]) for h in every]
            totals = [jnp.sum(probs[h], axis=1, keepdims=True) for h in every]
            scales = [1.0 / totals[h] for h in every]
            outs = [dot_nn(probs[h].astype(BF16), values[h]) * scales[h] for h in every]
            deltas = [
                jnp.sum(upstream[h].astype(F32) * outs[h], axis=1, keepdims=True) for h in every
            ]
            dscores = [(probs[h] * (dprobs[h] - deltas[h])).astype(BF16) for h in every]
            grads = [dot_nn(dscores[h], keys[h]) * (scales[h] * SCALE) for h in every]
            stats = jnp.zeros((BLOCK, BLOCK), F32)
            for h in every:
                stats = jnp.where(lane == h, peaks[h] + jnp.log2(totals[h]), stats)
                stats = jnp.where(lane == heads + h, deltas[h], stats)
            for h in every:
                out_ref[i, 0, :, head_of(h)] = outs[h].astype(BF16)
                out_ref[i, 1, :, head_of(h)] = grads[h].astype(BF16)
            stat_ref[i] = stats.T[: 2 * heads]

        by_width(cross_ref[i], width, body)
        return 0

    lax.fori_loop(0, qg_ref.shape[0], block, 0)


def key_kernel(
    width, heads, slot_ref, valid_ref, place_ref, cross_ref, count_ref, kv_ref, stat_ref, qg_local,
    below, above, ahead, rest, out_ref, pool, sem, extra_sem,
):
    fill_pool(count_ref[0], (qg_local, below, above), pool, (ahead, rest), sem, extra_sem)

    def block(j, _):
        def body(count):
            slots = [slot_ref[j, t] for t in range(count)]
            places = [place_ref[j, t] for t in range(count)]

            def log_tile(t, h):
                row = stat_ref[places[t], pl.ds(h, 1), :]
                return jnp.where(valid_ref[j, t] > 0, row, POS) if unsure(t) else row

            every = range(heads)
            queries = [jnp.concatenate([pool[s, 0, :, head_of(h)] for s in slots], axis=0) for h in every]
            upstream = [jnp.concatenate([pool[s, 1, :, head_of(h)] for s in slots], axis=0) for h in every]
            logs = [jnp.concatenate([log_tile(t, h) for t in range(count)], axis=1) for h in every]
            deltas = [
                jnp.concatenate([stat_ref[p, pl.ds(heads + h, 1), :] for p in places], axis=1)
                for h in every
            ]
            scores = [dot_nt(kv_ref[j, 0, :, head_of(h)], queries[h]) for h in every]
            dprobs = [dot_nt(kv_ref[j, 1, :, head_of(h)], upstream[h]) for h in every]
            probs = [jnp.exp2(scores[h] * SCALE2 - logs[h]) for h in every]
            dscores = [(probs[h] * (dprobs[h] - deltas[h])).astype(BF16) for h in every]
            grad_v = [dot_nn(probs[h].astype(BF16), upstream[h]) for h in every]
            grad_k = [dot_nn(dscores[h], queries[h]) * SCALE for h in every]
            for h in every:
                out_ref[j, 1, :, head_of(h)] = grad_v[h].astype(BF16)
                out_ref[j, 0, :, head_of(h)] = grad_k[h].astype(BF16)

        by_width(cross_ref[j], width, body)
        return 0

    lax.fori_loop(0, kv_ref.shape[0], block, 0)


def patterns_of(steps):
    groups, index = [], {}
    for d in range(1, steps):
        top = 1 << (d.bit_length() - 1)
        for low in range(top):
            pairs = [a for a in range(steps) if not a & top and a % top == low]
            for a in pairs:
                index[a, a ^ d] = index[a ^ d, a] = len(groups)
            groups.append([(a, a ^ d) for a in pairs] + [(a ^ d, a) for a in pairs])
    return groups, index


def tables(block_mask, spans, span_len, steps, groups):
    z = lax.axis_index("z")
    local = spans * SUB
    most = (spans * (spans - 1) + (WIDE - 1) * len(groups)) // WIDE
    capacity = WIDE * most
    iota = functools.partial(lax.broadcasted_iota, jnp.int32)
    as_int = lambda flags: flags.astype(jnp.int32)
    cube = block_mask.reshape(spans, span_len, spans, span_len)
    partner = jnp.sum(cube * (iota(cube.shape, 3) + 1), axis=3) - 1
    shape = partner.shape
    mine, spot, other = iota(shape, 0), iota(shape, 1), iota(shape, 2)
    linked = (partner >= 0) & (mine != other)
    here, there = spot // SUB, partner // SUB
    hop = jnp.where(linked, here ^ there, 0)
    top = sum(as_int(hop >= (1 << n)) << n for n in range(steps.bit_length()))
    top = (top + 1) // 2
    low = jnp.minimum(here, there) & (jnp.maximum(top, 1) - 1)
    group = jnp.where(hop > 0, base_of(hop, top) + low, -1)
    per_place = group.reshape(spans, steps, SUB, spans)
    numbers = iota((len(groups), spans, steps, SUB, spans), 0)
    messages = jnp.max(jnp.sum(as_int(per_place[None] == numbers), axis=(1, 3, 4)), axis=1)
    rounds = (messages + WIDE - 1) // WIDE
    number = iota((len(groups), len(groups)), 0)
    ends = jnp.sum(jnp.where(number <= iota(number.shape, 1), rounds[:, None], 0), axis=0)
    starts = ends - rounds
    total = jnp.sum(rounds)
    at = iota((most, len(groups)), 0)
    plan = jnp.minimum(jnp.sum(as_int(at >= ends[None]), axis=1), len(groups) - 1)
    left = jnp.sum(
        jnp.where(plan[:, None] == iota(at.shape, 1), messages[None] - WIDE * (at - starts[None]), 0), axis=1
    )
    plan = 2 * plan + as_int(left <= WIDE // 2)
    key = jnp.where(
        mine < other,
        (mine * span_len + spot) * spans + other,
        (other * span_len + partner) * spans + mine,
    )

    def at_place(table):
        return lax.dynamic_slice_in_dim(table, z * SUB, SUB, 1).reshape(local, spans)

    partner_l, linked_l, group_l, key_l = [at_place(t) for t in (partner, linked, group, key)]
    other_l = iota((local, spans), 1)
    block_l = iota((local, spans), 0)
    order = (group_l * (spans * span_len * spans) + key_l).reshape(-1)
    flat = group_l.reshape(-1)
    crossing = flat >= 0
    same = crossing[None, :] & (flat[None, :] == flat[:, None])
    rank = jnp.sum(as_int(same & (order[None, :] < order[:, None])), axis=1)
    first = jnp.sum(
        jnp.where(flat[:, None] == iota((local * spans, len(groups)), 1), starts[None], 0), axis=1
    )
    extra_slot = WIDE * first + rank
    hits = crossing[:, None] & (extra_slot[:, None] == iota((local * spans, capacity), 1))
    send_block = jnp.sum(as_int(hits) * block_l.reshape(-1)[:, None], axis=0).reshape(most, WIDE)
    for n in range(WIDE):
        plan = plan * local + send_block[:, n]
    cross_slot = jnp.where(
        group_l >= 0,
        local + 2 * spans + extra_slot.reshape(local, spans),
        other_l * SUB + partner_l % SUB,
    )
    cross_place = (z ^ (partner_l // SUB)) * local + other_l * SUB + partner_l % SUB
    own = block_l[:, :1]
    span_l, x_l = own // SUB, own % SUB
    pair = own + 1 - 2 * x_l
    near_slot = jnp.where(x_l == 0, local + span_l, local + spans + span_l)
    near_ok = jnp.where(x_l == 0, z > 0, z < steps - 1)
    near_place = jnp.where(x_l == 0, (z ^ (z - 1)) * local + own + 1, (z ^ (z + 1)) * local + own - 1)
    before = iota((local, spans, spans), 2) < iota((local, spans, spans), 1)
    position = jnp.sum(as_int(linked_l[:, None, :] & before), axis=2)
    chosen = linked_l[:, None, :] & (position[:, None, :] == iota((local, spans - 1, spans), 1))

    def pick(table):
        return jnp.sum(jnp.where(chosen, table[:, None, :], 0), axis=2)

    sure = jnp.ones_like(own)
    ok = jnp.concatenate([sure, sure, as_int(near_ok), pick(as_int(linked_l))], axis=1)
    slot = jnp.concatenate([own, pair, near_slot, pick(cross_slot)], axis=1)
    place = jnp.concatenate([own, pair, near_place, pick(cross_place)], axis=1)
    slot = jnp.where(ok > 0, slot, own)
    place = jnp.where(ok > 0, place, own)
    cross = jnp.sum(as_int(linked_l), axis=1)
    return slot, ok, place, cross, total, plan, capacity


def base_of(hop, top):
    smaller = (top * top - 1) // 3
    return smaller + (hop - top) * top


def shards(query_tokens, key_tokens, value_tokens, cotangent, block_mask):
    spans = lax.axis_size("blk")
    steps = lax.axis_size("z")
    span_len = steps * SUB
    local = spans * SUB
    groups, _ = patterns_of(steps)

    def exchange(pair):
        return lax.all_to_all(pair, ("blk", "x"), split_axis=0, concat_axis=0, tiled=True)

    kv = exchange(pack(key_tokens, value_tokens, local))
    qg = exchange(pack(query_tokens, cotangent, local))
    columns = kv.shape[3]
    heads = columns // HEAD_DIM
    slot, ok, place, cross, total, plan, capacity = tables(
        block_mask, spans, span_len, steps, groups
    )
    width = slot.shape[1]
    upward = [(n, n + 1) for n in range(steps - 1)]
    downward = [(n + 1, n) for n in range(steps - 1)]

    def neighbours(pair):
        edges = pair.reshape(spans, SUB, 2, BLOCK, columns)
        below = lax.ppermute(edges[:, SUB - 1], "z", upward)
        above = lax.ppermute(edges[:, 0], "z", downward)
        return below, above

    kv_below, kv_above = neighbours(kv)
    qg_below, qg_above = neighbours(qg)

    def take(code):
        picks = []
        for _ in range(WIDE):
            picks.insert(0, code % local)
            code = code // local
        return code, picks

    def swap(pair, *picks, group, size):
        sent = jnp.concatenate([lax.dynamic_slice_in_dim(pair, n, 1, 0) for n in picks[:size]])
        got = lax.ppermute(sent, "z", group)
        return jnp.concatenate([got] * (WIDE // size))

    swaps = [
        lambda pair, *picks, g=g, n=n: swap(pair, *picks, group=g, size=n)
        for g in groups
        for n in (WIDE, WIDE // 2)
    ]
    blank = functools.partial(
        pl.pallas_call,
        lambda out_ref: None,
        out_specs=pl.BlockSpec(memory_space=pl.ANY),
        compiler_params=pltpu.CompilerParams(vmem_limit_bytes=1 << 20),
        name="extra_blocks",
    )

    def crossing(pair):
        size = (WIDE, 2, BLOCK, columns)
        unused = blank(out_shape=jax.ShapeDtypeStruct(size, BF16))()
        buffer = blank(out_shape=jax.ShapeDtypeStruct((capacity - WIDE,) + size[1:], BF16))()

        def one_round(r, held):
            code, picks = take(plan[r])
            got = lax.switch(code, swaps, pair, *picks)
            return lax.dynamic_update_slice_in_dim(held, got, WIDE * (r - 1), 0)

        code, picks = take(plan[0])
        skip = [lambda held, pair, *picks: held]
        some = [lambda held, pair, *picks, f=f: f(pair, *picks) for f in swaps]
        ahead = lax.switch(
            jnp.where(total > 0, code + 1, 0), skip + some, unused, pair, *picks
        )
        return ahead, lax.fori_loop(1, total, one_round, buffer)

    kv_extra = crossing(kv)
    count = WIDE * total.reshape(1)

    smem = pl.BlockSpec(memory_space=pltpu.SMEM)
    vmem = pl.BlockSpec(memory_space=pltpu.VMEM)
    anywhere = pl.BlockSpec(memory_space=pl.ANY)
    scratch = [
        pltpu.VMEM((local + 2 * spans + capacity, 2, BLOCK, columns), BF16),
        pltpu.SemaphoreType.DMA((3,)),
        pltpu.SemaphoreType.DMA((capacity,)),
    ]
    block_bytes = 2 * 2 * BLOCK * columns
    grant = block_bytes * (capacity + 2 * spans + 6 * local) + (10 << 20)
    cost = pl.CostEstimate(
        flops=2 * 4 * local * heads * width * BLOCK * BLOCK * HEAD_DIM,
        bytes_accessed=16 * local * BLOCK * columns,
        transcendentals=local * heads * width * BLOCK * BLOCK,
    )
    out_pair, stats = pl.pallas_call(
        functools.partial(query_kernel, width, heads),
        out_shape=(
            jax.ShapeDtypeStruct(qg.shape, BF16),
            jax.ShapeDtypeStruct((local, 2 * heads, BLOCK), F32),
        ),
        in_specs=[smem] * 4 + [vmem] + [anywhere] * 5,
        out_specs=(vmem, vmem),
        scratch_shapes=scratch,
        cost_estimate=cost,
        compiler_params=pltpu.CompilerParams(vmem_limit_bytes=grant),
        name="query_pass",
    )(slot, ok, cross, count, qg, kv, kv_below, kv_above, *kv_extra)
    far = [lax.ppermute(stats, "z", [(n, n ^ d) for n in range(steps)]) for d in range(1, steps)]
    all_stats = jnp.concatenate([stats] + far)
    qg_extra = crossing(qg)
    grad_pair = pl.pallas_call(
        functools.partial(key_kernel, width, heads),
        out_shape=jax.ShapeDtypeStruct(kv.shape, BF16),
        in_specs=[smem] * 5 + [vmem, vmem] + [anywhere] * 5,
        out_specs=vmem,
        scratch_shapes=scratch,
        cost_estimate=cost,
        compiler_params=pltpu.CompilerParams(vmem_limit_bytes=grant),
        name="key_pass",
    )(slot, ok, place, cross, count, kv, all_stats, qg, qg_below, qg_above, *qg_extra)
    out_back = exchange(out_pair)
    grad_back = exchange(grad_pair)
    attended, grad_query = unpack(out_back)
    grad_key, grad_value = unpack(grad_back)
    return attended, grad_query, grad_key, grad_value


def solution(mesh):
    spans, ulysses = mesh.shape["blk"], mesh.shape["ulysses"]
    split = Mesh(mesh.devices.reshape(spans, ulysses // SUB, SUB), ("blk", "z", "x"))
    tokens = P(("blk", "z", "x"), None)
    return jax.shard_map(
        shards,
        mesh=split,
        in_specs=(tokens, tokens, tokens, tokens, P()),
        out_specs=(tokens, tokens, tokens, tokens),
        check_vma=False,
    )
```

```python
import functools
import math
import jax
import jax.numpy as jnp
from jax import lax
from jax.experimental import pallas as pl
from jax.experimental.pallas import tpu as pltpu
from jax.sharding import Mesh, PartitionSpec as P

HEAD_DIM = 128
BLOCK = 128
SUB = 2
NEG = float("-inf")
POS = float("inf")
BF16 = jnp.bfloat16
F32 = jnp.float32
SCALE = HEAD_DIM ** (-0.5)
SCALE2 = SCALE * math.log2(math.e)
OWN = 3
WIDE = 4


def head_of(h):
    return slice(h * HEAD_DIM, (h + 1) * HEAD_DIM)


def dot_nt(a, b):
    return lax.dot_general(a, b, (((1,), (1,)), ((), ())), preferred_element_type=F32)


def dot_nn(a, b):
    return lax.dot_general(a, b, (((1,), (0,)), ((), ())), preferred_element_type=F32)


def pack_kernel(a_ref, b_ref, out_ref, held, in_sem, out_sem):
    groups, _, _, columns = out_ref.shape
    arrive, leave = [], []
    for c in range(groups):
        for n, source in enumerate((a_ref, b_ref)):
            arrive.append(
                pltpu.make_async_copy(
                    source.at[:, c * columns : (c + 1) * columns], held.at[c, n], in_sem.at[c, n]
                )
            )
            leave.append(pltpu.make_async_copy(held.at[c, n], out_ref.at[c, n], out_sem.at[c, n]))
    for copy in arrive:
        copy.start()
    for first, second in zip(arrive, leave):
        first.wait()
        second.start()
    for copy in leave:
        copy.wait()


def unpack_kernel(in_ref, a_ref, b_ref, sem):
    groups, _, _, columns = in_ref.shape
    copies = [
        pltpu.make_async_copy(
            in_ref.at[c, n], target.at[:, c * columns : (c + 1) * columns], sem.at[c, n]
        )
        for c in range(groups)
        for n, target in enumerate((a_ref, b_ref))
    ]
    for copy in copies:
        copy.start()
    for copy in copies:
        copy.wait()


def pack(a, b, groups):
    rows, columns = a.shape
    shape = (groups, 2, rows, columns // groups)
    anywhere = pl.BlockSpec(memory_space=pl.ANY)
    return pl.pallas_call(
        pack_kernel,
        out_shape=jax.ShapeDtypeStruct(shape, a.dtype),
        in_specs=[anywhere] * 2,
        out_specs=anywhere,
        scratch_shapes=[
            pltpu.VMEM(shape, a.dtype),
            pltpu.SemaphoreType.DMA((groups, 2)),
            pltpu.SemaphoreType.DMA((groups, 2)),
        ],
        name="pack",
    )(a, b)


def unpack(pair):
    groups, _, rows, columns = pair.shape
    anywhere = pl.BlockSpec(memory_space=pl.ANY)
    flat = jax.ShapeDtypeStruct((rows, groups * columns), pair.dtype)
    return pl.pallas_call(
        unpack_kernel,
        out_shape=(flat, flat),
        in_specs=[pl.BlockSpec(memory_space=pltpu.VMEM)],
        out_specs=(anywhere, anywhere),
        scratch_shapes=[pltpu.SemaphoreType.DMA((groups, 2))],
        compiler_params=pltpu.CompilerParams(vmem_limit_bytes=5 * rows * groups * columns),
        name="unpack",
    )(pair)


def fill_pool(count, parts, pool, extra, sem, extra_sem):
    copies = []
    start = 0
    for m, source in enumerate(parts):
        size = source.shape[0]
        copies.append(pltpu.make_async_copy(source, pool.at[pl.ds(start, size)], sem.at[m]))
        start += size
    for copy in copies:
        copy.start()

    ahead, rest = extra
    early = ahead.shape[0]

    def move(slot):
        return pltpu.make_async_copy(rest.at[slot - early], pool.at[start + slot], extra_sem.at[slot])

    def move_ahead():
        return pltpu.make_async_copy(ahead, pool.at[pl.ds(start, early)], extra_sem.at[0])

    @pl.when(count > 0)
    def _():
        move_ahead().start()

    lax.fori_loop(early, count, lambda slot, _: (move(slot).start(), 0)[1], 0)
    for copy in copies:
        copy.wait()

    @pl.when(count > 0)
    def _():
        move_ahead().wait()

    lax.fori_loop(early, count, lambda slot, _: (move(slot).wait(), 0)[1], 0)


def by_width(cross, width, body):
    top = min(OWN, width - OWN)
    for n in range(top):

        @pl.when(cross == n)
        def _(n=n):
            body(OWN + n)

    @pl.when(cross >= top)
    def _():
        body(width)


def unsure(t):
    return t == OWN - 1 or t >= 2 * OWN


def query_kernel(
    width, heads, slot_ref, valid_ref, cross_ref, count_ref, qg_ref, kv_local, below, above, ahead, rest,
    out_ref, stat_ref, pool, sem, extra_sem,
):
    fill_pool(count_ref[0], (kv_local, below, above), pool, (ahead, rest), sem, extra_sem)
    lane = lax.broadcasted_iota(jnp.int32, (BLOCK, BLOCK), 1)

    def block(i, _):
        def body(count):
            slots = [slot_ref[i, t] for t in range(count)]
            bias = jnp.concatenate(
                [
                    jnp.full((1, BLOCK), jnp.where(valid_ref[i, t] > 0, 0.0, NEG), F32)
                    if unsure(t)
                    else jnp.zeros((1, BLOCK), F32)
                    for t in range(count)
                ],
                axis=1,
            )
            every = range(heads)
            keys = [jnp.concatenate([pool[s, 0, :, head_of(h)] for s in slots], axis=0) for h in every]
            values = [jnp.concatenate([pool[s, 1, :, head_of(h)] for s in slots], axis=0) for h in every]
            upstream = [qg_ref[i, 1, :, head_of(h)] for h in every]
            scores = [dot_nt(qg_ref[i, 0, :, head_of(h)], keys[h]) * SCALE2 + bias for h in every]
            dprobs = [dot_nt(upstream[h], values[h]) for h in every]
            peaks = [jnp.max(scores[h], axis=1, keepdims=True) for h in every]
            probs = [jnp.exp2(scores[h] - peaks[h]) for h in every]
            totals = [jnp.sum(probs[h], axis=1, keepdims=True) for h in every]
            scales = [1.0 / totals[h] for h in every]
            outs = [dot_nn(probs[h].astype(BF16), values[h]) * scales[h] for h in every]
            deltas = [
                jnp.sum(upstream[h].astype(F32) * outs[h], axis=1, keepdims=True) for h in every
            ]
            dscores = [(probs[h] * (dprobs[h] - deltas[h])).astype(BF16) for h in every]
            grads = [dot_nn(dscores[h], keys[h]) * (scales[h] * SCALE) for h in every]
            stats = jnp.zeros((BLOCK, BLOCK), F32)
            for h in every:
                stats = jnp.where(lane == h, peaks[h] + jnp.log2(totals[h]), stats)
                stats = jnp.where(lane == heads + h, deltas[h], stats)
            for h in every:
                out_ref[i, 0, :, head_of(h)] = outs[h].astype(BF16)
                out_ref[i, 1, :, head_of(h)] = grads[h].astype(BF16)
            stat_ref[i] = stats.T[: 2 * heads]

        by_width(cross_ref[i], width, body)
        return 0

    lax.fori_loop(0, qg_ref.shape[0], block, 0)


def key_kernel(
    width, heads, slot_ref, valid_ref, place_ref, cross_ref, count_ref, kv_ref, stat_ref, qg_local,
    below, above, ahead, rest, out_ref, pool, sem, extra_sem,
):
    fill_pool(count_ref[0], (qg_local, below, above), pool, (ahead, rest), sem, extra_sem)

    def block(j, _):
        def body(count):
            slots = [slot_ref[j, t] for t in range(count)]
            places = [place_ref[j, t] for t in range(count)]

            def log_tile(t, h):
                row = stat_ref[places[t], pl.ds(h, 1), :]
                return jnp.where(valid_ref[j, t] > 0, row, POS) if unsure(t) else row

            every = range(heads)
            queries = [jnp.concatenate([pool[s, 0, :, head_of(h)] for s in slots], axis=0) for h in every]
            upstream = [jnp.concatenate([pool[s, 1, :, head_of(h)] for s in slots], axis=0) for h in every]
            logs = [jnp.concatenate([log_tile(t, h) for t in range(count)], axis=1) for h in every]
            deltas = [
                jnp.concatenate([stat_ref[p, pl.ds(heads + h, 1), :] for p in places], axis=1)
                for h in every
            ]
            scores = [dot_nt(kv_ref[j, 0, :, head_of(h)], queries[h]) for h in every]
            dprobs = [dot_nt(kv_ref[j, 1, :, head_of(h)], upstream[h]) for h in every]
            probs = [jnp.exp2(scores[h] * SCALE2 - logs[h]) for h in every]
            dscores = [(probs[h] * (dprobs[h] - deltas[h])).astype(BF16) for h in every]
            grad_v = [dot_nn(probs[h].astype(BF16), upstream[h]) for h in every]
            grad_k = [dot_nn(dscores[h], queries[h]) * SCALE for h in every]
            for h in every:
                out_ref[j, 1, :, head_of(h)] = grad_v[h].astype(BF16)
                out_ref[j, 0, :, head_of(h)] = grad_k[h].astype(BF16)

        by_width(cross_ref[j], width, body)
        return 0

    lax.fori_loop(0, kv_ref.shape[0], block, 0)


def patterns_of(steps):
    groups, sizes, joined = [], [], []
    for d in range(1, steps):
        top = 1 << (d.bit_length() - 1)
        for low in range(top):
            pairs = [a for a in range(steps) if not a & top and a % top == low]
            if d == 2:
                joined.append(len(groups))
            groups.append([(a, a ^ d) for a in pairs] + [(a ^ d, a) for a in pairs])
            sizes.append((WIDE, WIDE // 2) if d < 3 else (WIDE,))
    if joined:
        groups.append(sum((groups[g] for g in joined), []))
        sizes.append((WIDE // 2,))
    return groups, sizes, joined


def tables(block_mask, spans, span_len, steps, groups, sizes, joined):
    z = lax.axis_index("z")
    local = spans * SUB
    most = (spans * (spans - 1) + (WIDE - 1) * len(groups)) // WIDE
    capacity = WIDE * most
    iota = functools.partial(lax.broadcasted_iota, jnp.int32)
    as_int = lambda flags: flags.astype(jnp.int32)
    cube = block_mask.reshape(spans, span_len, spans, span_len)
    partner = jnp.sum(cube * (iota(cube.shape, 3) + 1), axis=3) - 1
    shape = partner.shape
    mine, spot, other = iota(shape, 0), iota(shape, 1), iota(shape, 2)
    linked = (partner >= 0) & (mine != other)
    here, there = spot // SUB, partner // SUB
    hop = jnp.where(linked, here ^ there, 0)
    top = sum(as_int(hop >= (1 << n)) << n for n in range(steps.bit_length()))
    top = (top + 1) // 2
    low = jnp.minimum(here, there) & (jnp.maximum(top, 1) - 1)
    group = jnp.where(hop > 0, base_of(hop, top) + low, -1)
    per_place = group.reshape(spans, steps, SUB, spans)
    numbers = iota((len(groups), spans, steps, SUB, spans), 0)
    messages = jnp.max(jnp.sum(as_int(per_place[None] == numbers), axis=(1, 3, 4)), axis=1)
    if joined:
        one, two = joined
        small = jnp.maximum(messages[one], messages[two])
        join = (jnp.minimum(messages[one], messages[two]) > 0) & (small <= WIDE // 2)
        member = iota(messages.shape, 0)
        in_pair = (member == one) | (member == two)
        messages = jnp.where(join & in_pair, 0, messages)
        messages = jnp.where(join & (member == len(groups) - 1), small, messages)
        group = jnp.where(join & ((group == one) | (group == two)), len(groups) - 1, group)
    rounds = (messages + WIDE - 1) // WIDE
    number = iota((len(groups), len(groups)), 0)
    ends = jnp.sum(jnp.where(number <= iota(number.shape, 1), rounds[:, None], 0), axis=0)
    starts = ends - rounds
    total = jnp.sum(rounds)
    at = iota((most, len(groups)), 0)
    plan = jnp.minimum(jnp.sum(as_int(at >= ends[None]), axis=1), len(groups) - 1)
    left = jnp.sum(
        jnp.where(plan[:, None] == iota(at.shape, 1), messages[None] - WIDE * (at - starts[None]), 0), axis=1
    )
    base = 0
    move = jnp.zeros_like(plan)
    for g, allowed in enumerate(sizes):
        choice = base + (as_int(left <= WIDE // 2) if len(allowed) > 1 else 0)
        move = jnp.where(plan == g, choice, move)
        base += len(allowed)
    plan = move
    key = jnp.where(
        mine < other,
        (mine * span_len + spot) * spans + other,
        (other * span_len + partner) * spans + mine,
    )

    def at_place(table):
        return lax.dynamic_slice_in_dim(table, z * SUB, SUB, 1).reshape(local, spans)

    partner_l, linked_l, group_l, key_l = [at_place(t) for t in (partner, linked, group, key)]
    other_l = iota((local, spans), 1)
    block_l = iota((local, spans), 0)
    order = (group_l * (spans * span_len * spans) + key_l).reshape(-1)
    flat = group_l.reshape(-1)
    crossing = flat >= 0
    same = crossing[None, :] & (flat[None, :] == flat[:, None])
    rank = jnp.sum(as_int(same & (order[None, :] < order[:, None])), axis=1)
    first = jnp.sum(
        jnp.where(flat[:, None] == iota((local * spans, len(groups)), 1), starts[None], 0), axis=1
    )
    extra_slot = WIDE * first + rank
    hits = crossing[:, None] & (extra_slot[:, None] == iota((local * spans, capacity), 1))
    send_block = jnp.sum(as_int(hits) * block_l.reshape(-1)[:, None], axis=0).reshape(most, WIDE)
    for n in range(WIDE):
        plan = plan * local + send_block[:, n]
    cross_slot = jnp.where(
        group_l >= 0,
        local + 2 * spans + extra_slot.reshape(local, spans),
        other_l * SUB + partner_l % SUB,
    )
    cross_place = (z ^ (partner_l // SUB)) * local + other_l * SUB + partner_l % SUB
    own = block_l[:, :1]
    span_l, x_l = own // SUB, own % SUB
    pair = own + 1 - 2 * x_l
    near_slot = jnp.where(x_l == 0, local + span_l, local + spans + span_l)
    near_ok = jnp.where(x_l == 0, z > 0, z < steps - 1)
    near_place = jnp.where(x_l == 0, (z ^ (z - 1)) * local + own + 1, (z ^ (z + 1)) * local + own - 1)
    before = iota((local, spans, spans), 2) < iota((local, spans, spans), 1)
    position = jnp.sum(as_int(linked_l[:, None, :] & before), axis=2)
    chosen = linked_l[:, None, :] & (position[:, None, :] == iota((local, spans - 1, spans), 1))

    def pick(table):
        return jnp.sum(jnp.where(chosen, table[:, None, :], 0), axis=2)

    sure = jnp.ones_like(own)
    ok = jnp.concatenate([sure, sure, as_int(near_ok), pick(as_int(linked_l))], axis=1)
    slot = jnp.concatenate([own, pair, near_slot, pick(cross_slot)], axis=1)
    place = jnp.concatenate([own, pair, near_place, pick(cross_place)], axis=1)
    slot = jnp.where(ok > 0, slot, own)
    place = jnp.where(ok > 0, place, own)
    cross = jnp.sum(as_int(linked_l), axis=1)
    return slot, ok, place, cross, total, plan, capacity


def base_of(hop, top):
    smaller = (top * top - 1) // 3
    return smaller + (hop - top) * top


def shards(query_tokens, key_tokens, value_tokens, cotangent, block_mask):
    spans = lax.axis_size("blk")
    steps = lax.axis_size("z")
    span_len = steps * SUB
    local = spans * SUB
    groups, sizes, joined = patterns_of(steps)

    def exchange(pair):
        return lax.all_to_all(pair, ("blk", "x"), split_axis=0, concat_axis=0, tiled=True)

    kv = exchange(pack(key_tokens, value_tokens, local))
    qg = exchange(pack(query_tokens, cotangent, local))
    columns = kv.shape[3]
    heads = columns // HEAD_DIM
    slot, ok, place, cross, total, plan, capacity = tables(block_mask, spans, span_len, steps, groups, sizes, joined)
    width = slot.shape[1]
    upward = [(n, n + 1) for n in range(steps - 1)]
    downward = [(n + 1, n) for n in range(steps - 1)]

    def neighbours(pair):
        edges = pair.reshape(spans, SUB, 2, BLOCK, columns)
        below = lax.ppermute(edges[:, SUB - 1], "z", upward)
        above = lax.ppermute(edges[:, 0], "z", downward)
        return below, above

    kv_below, kv_above = neighbours(kv)
    qg_below, qg_above = neighbours(qg)

    def take(code):
        picks = []
        for _ in range(WIDE):
            picks.insert(0, code % local)
            code = code // local
        return code, picks

    def swap(pair, *picks, group, size):
        sent = jnp.concatenate([lax.dynamic_slice_in_dim(pair, n, 1, 0) for n in picks[:size]])
        got = lax.ppermute(sent, "z", group)
        return jnp.concatenate([got] * (WIDE // size))

    swaps = [
        lambda pair, *picks, g=g, n=n: swap(pair, *picks, group=g, size=n)
        for g, allowed in zip(groups, sizes)
        for n in allowed
    ]
    blank = functools.partial(
        pl.pallas_call,
        lambda out_ref: None,
        out_specs=pl.BlockSpec(memory_space=pl.ANY),
        compiler_params=pltpu.CompilerParams(vmem_limit_bytes=1 << 20),
        name="extra_blocks",
    )

    def crossing(pair):
        size = (WIDE, 2, BLOCK, columns)
        unused = blank(out_shape=jax.ShapeDtypeStruct(size, BF16))()
        buffer = blank(out_shape=jax.ShapeDtypeStruct((capacity - WIDE,) + size[1:], BF16))()

        def one_round(r, held):
            code, picks = take(plan[r])
            got = lax.switch(code, swaps, pair, *picks)
            return lax.dynamic_update_slice_in_dim(held, got, WIDE * (r - 1), 0)

        code, picks = take(plan[0])
        skip = [lambda held, pair, *picks: held]
        some = [lambda held, pair, *picks, f=f: f(pair, *picks) for f in swaps]
        ahead = lax.switch(
            jnp.where(total > 0, code + 1, 0), skip + some, unused, pair, *picks
        )
        return ahead, lax.fori_loop(1, total, one_round, buffer)

    kv_extra = crossing(kv)
    count = WIDE * total.reshape(1)

    smem = pl.BlockSpec(memory_space=pltpu.SMEM)
    vmem = pl.BlockSpec(memory_space=pltpu.VMEM)
    anywhere = pl.BlockSpec(memory_space=pl.ANY)
    scratch = [
        pltpu.VMEM((local + 2 * spans + capacity, 2, BLOCK, columns), BF16),
        pltpu.SemaphoreType.DMA((3,)),
        pltpu.SemaphoreType.DMA((capacity,)),
    ]
    block_bytes = 2 * 2 * BLOCK * columns
    grant = block_bytes * (capacity + 2 * spans + 6 * local) + (10 << 20)
    cost = pl.CostEstimate(
        flops=2 * 4 * local * heads * width * BLOCK * BLOCK * HEAD_DIM,
        bytes_accessed=16 * local * BLOCK * columns,
        transcendentals=local * heads * width * BLOCK * BLOCK,
    )
    out_pair, stats = pl.pallas_call(
        functools.partial(query_kernel, width, heads),
        out_shape=(
            jax.ShapeDtypeStruct(qg.shape, BF16),
            jax.ShapeDtypeStruct((local, 2 * heads, BLOCK), F32),
        ),
        in_specs=[smem] * 4 + [vmem] + [anywhere] * 5,
        out_specs=(vmem, vmem),
        scratch_shapes=scratch,
        cost_estimate=cost,
        compiler_params=pltpu.CompilerParams(vmem_limit_bytes=grant),
        name="query_pass",
    )(slot, ok, cross, count, qg, kv, kv_below, kv_above, *kv_extra)
    far = [lax.ppermute(stats, "z", [(n, n ^ d) for n in range(steps)]) for d in range(1, steps)]
    all_stats = jnp.concatenate([stats] + far)
    qg_extra = crossing(qg)
    grad_pair = pl.pallas_call(
        functools.partial(key_kernel, width, heads),
        out_shape=jax.ShapeDtypeStruct(kv.shape, BF16),
        in_specs=[smem] * 5 + [vmem, vmem] + [anywhere] * 5,
        out_specs=vmem,
        scratch_shapes=scratch,
        cost_estimate=cost,
        compiler_params=pltpu.CompilerParams(vmem_limit_bytes=grant),
        name="key_pass",
    )(slot, ok, place, cross, count, kv, all_stats, qg, qg_below, qg_above, *qg_extra)
    out_back = exchange(out_pair)
    grad_back = exchange(grad_pair)
    attended, grad_query = unpack(out_back)
    grad_key, grad_value = unpack(grad_back)
    return attended, grad_query, grad_key, grad_value


def solution(mesh):
    spans, ulysses = mesh.shape["blk"], mesh.shape["ulysses"]
    split = Mesh(mesh.devices.reshape(spans, ulysses // SUB, SUB), ("blk", "z", "x"))
    tokens = P(("blk", "z", "x"), None)
    return jax.shard_map(
        shards,
        mesh=split,
        in_specs=(tokens, tokens, tokens, tokens, P()),
        out_specs=(tokens, tokens, tokens, tokens),
        check_vma=False,
    )
```
